256 devices in a mesh: sec: 4 (over y_hi, core), row: 4 (over x), col: 16 (over z, y_lo).
Axes of the slice: x: 4, y: 4 (y_hi: 2, y_lo: 2; y = y_hi * 2 + y_lo), z: 8, core: 2. Of those that a mesh axis runs over, the one named last changes fastest.
Arguments:
- images: float32 [4, 1024, 4096], P('sec', 'row', 'col'), may hold values from -6 to 6
- stiffness: float32 [4, 1024, 4096], P('sec', 'row', 'col'), may hold values from 0.1 to 1
Outputs:
- tensor: float32 [5, 4, 1024, 4096], P(None, 'sec', 'row', 'col')
- field: float32 [2, 4, 1024, 4096], P(None, 'sec', 'row', 'col')
The draws below stay inside these ranges and needn't reach their ends.
All inputs are finite; a program needn't handle non-finite values.
Results may differ from the reference program's by a relative error of at most 0.00002.
Values sent between devices are 32-bit elements; how exact they have to be, the bound alone decides.
No kernel may reach another device: no remote copies, remote signals or barrier semaphores. Data moves between devices by JAX's collectives and lax.ppermute only.
A program may use at most 64 MiB of HBM per device.

```python
import math
import jax
import jax.numpy as jnp

RADIUS = 4
SWEEPS = 4
ROUNDS = 2
SECTIONS = 4
HEIGHT = 1024
WIDTH = 4096


def steps_of(rng, extent, pieces, least, high):
    def one(position, blocks):
        heights = jax.random.uniform(jax.random.fold_in(jax.random.fold_in(rng, 6), position), (blocks,), jnp.float32, least / len(pieces), high / len(pieces))
        return jnp.repeat(jnp.exp(heights), extent[position] // blocks).reshape((-1,) + (1,) * (len(extent) - position - 1))

    factor_of = one(*pieces[0])
    for cut in pieces[1:]:
        factor_of = factor_of * one(*cut)
    return factor_of


def scatter_about(key, shape, width, reach, cuts=(), held_as=jnp.bfloat16):
    array = width * jax.random.normal(key, shape, jnp.float32)
    if cuts:
        array = array * steps_of(key, shape, cuts, -0.22, 0.18)
    return jnp.clip(array, -reach, reach).astype(held_as)


def setup_inputs(seed: int = 0) -> dict:
    seeds = jax.random.split(jax.random.key(seed), 3)
    return {
        "images": scatter_about(seeds[0], (SECTIONS, HEIGHT, WIDTH), 1.0, 6.0, ((0, 4), (1, 4), (2, 16)), jnp.float32),
        "stiffness": jnp.clip(jnp.exp(math.log(1.0) - 2.3025851 * jax.random.uniform(seeds[1], (SECTIONS, HEIGHT, WIDTH), jnp.float32) ** steps_of(seeds[1], (SECTIONS, HEIGHT, WIDTH), ((0, 4), (1, 4), (2, 16)), -0.2, 0.2)), 0.1, 1.0),
    }


coupling = 0.25

def gradients(padded):
    grad_y = (padded[..., 2:, 1:-1] - padded[..., :-2, 1:-1]) * 0.5
    grad_x = (padded[..., 1:-1, 2:] - padded[..., 1:-1, :-2]) * 0.5
    return (grad_y, grad_x)

def products(grad_y, grad_x, change):
    return jnp.stack([grad_x * grad_x, grad_x * grad_y, grad_y * grad_y, grad_x * change, grad_y * change])

def window_mean(widened, radius):
    row_count = widened.shape[-2] - 2 * radius
    col_count = widened.shape[-1] - 2 * radius
    partial_rows = widened[..., 0:row_count, :]
    for offset in range(1, 2 * radius + 1):
        partial_rows = partial_rows + widened[..., offset:offset + row_count, :]
    summed = partial_rows[..., 0:col_count]
    for offset in range(1, 2 * radius + 1):
        summed = summed + partial_rows[..., offset:offset + col_count]
    return summed / float((2 * radius + 1) ** 2)

def couplings(stiff_pad):
    centre = stiff_pad[..., 1:-1, 1:-1]
    kappa_up = jnp.sqrt(centre * stiff_pad[..., :-2, 1:-1])
    kappa_down = jnp.sqrt(centre * stiff_pad[..., 2:, 1:-1])
    kappa_left = jnp.sqrt(centre * stiff_pad[..., 1:-1, :-2])
    kappa_right = jnp.sqrt(centre * stiff_pad[..., 1:-1, 2:])
    kappa_sum = kappa_up + kappa_down + kappa_left + kappa_right
    return ((kappa_up, kappa_down, kappa_left, kappa_right), kappa_sum)

def jacobi(field_pad, kappas, kappa_sum, tensor, beside):
    neighbour = kappas[0] * field_pad[..., :-2, 1:-1] + kappas[1] * field_pad[..., 2:, 1:-1]
    neighbour = neighbour + kappas[2] * field_pad[..., 1:-1, :-2] + kappas[3] * field_pad[..., 1:-1, 2:]
    diagonal = kappa_sum + 2.0 * coupling
    first_diag = tensor[0] + diagonal
    second_diag = tensor[2] + diagonal
    off_diag = tensor[1]
    determinant = first_diag * second_diag - off_diag * off_diag
    right_x = coupling * beside[0] + neighbour[0] - tensor[3]
    right_y = coupling * beside[1] + neighbour[1] - tensor[4]
    new_x = (second_diag * right_x - off_diag * right_y) / determinant
    new_y = (first_diag * right_y - off_diag * right_x) / determinant
    return jnp.stack([new_x, new_y])

def reference(images, stiffness):
    section_count = images.shape[0]
    later = jnp.concatenate([images[1:], jnp.zeros_like(images[:1])], axis=0)
    padded = jnp.pad(images, ((0, 0), (1, 1), (1, 1)))
    grad_y, grad_x = gradients(padded)
    stacked = products(grad_y, grad_x, later - images)
    widened = jnp.pad(stacked, ((0, 0), (0, 0), (RADIUS, RADIUS), (RADIUS, RADIUS)))
    tensor = window_mean(widened, RADIUS)
    keep = (jnp.arange(section_count) < section_count - 1).astype(tensor.dtype)
    tensor = tensor * keep[None, :, None, None]
    stiff_pad = jnp.pad(stiffness, ((0, 0), (1, 1), (1, 1)))
    kappas, kappa_sum = couplings(stiff_pad)
    field = jnp.zeros((2,) + images.shape, images.dtype)
    for round_index in range(ROUNDS):
        if round_index == 0:
            beside = jnp.zeros_like(field)
        else:
            below_part = jnp.concatenate([jnp.zeros_like(field[:, :1]), field[:, :-1]], axis=1)
            above_part = jnp.concatenate([field[:, 1:], jnp.zeros_like(field[:, :1])], axis=1)
            beside = below_part + above_part
        for sweep_index in range(SWEEPS):
            field_pad = jnp.pad(field, ((0, 0), (0, 0), (1, 1), (1, 1)))
            field = jacobi(field_pad, kappas, kappa_sum, tensor, beside)
    return (tensor, field)
```

```python
import jax
import jax.numpy as jnp
from jax import lax
from jax.experimental import pallas as pl
from jax.experimental.pallas import tpu as pltpu
from jax.sharding import PartitionSpec as P

RADIUS = 4
COUPLING = 0.25
AXES = ("sec", "row", "col")

TILE = 256
RIM = 16
EXT = TILE + 2 * RIM
BLOCKS = EXT // 8
INNER = BLOCKS - 2
GROUP = 5
FIELD_RIM = 8


def even(i, count):
    j = i ^ 1
    return j if j < count else None


def odd(i, count):
    j = ((i + 1) ^ 1) - 1
    return j if 0 <= j < count else None


def same(i, count):
    return i


def pairs(sec_of, row_of, col_of):
    secs, rows, cols = (lax.axis_size(name) for name in AXES)
    found = []
    for s in range(secs):
        for r in range(rows):
            for c in range(cols):
                to = (sec_of(s, secs), row_of(r, rows), col_of(c, cols))
                if None not in to:
                    found.append(((s * rows + r) * cols + c, (to[0] * rows + to[1]) * cols + to[2]))
    return found


def send(value, sec_of=same, row_of=same, col_of=same):
    return lax.ppermute(value, AXES, pairs(sec_of, row_of, col_of))


def earlier(s, count):
    return s - 1 if s > 0 else None


def lanes():
    return lax.broadcasted_iota(jnp.int32, (8, 128), 1)


def from_left(tiles, steps):
    rolled = [pltpu.roll(t, steps, 1) for t in tiles]
    edge = lanes() < steps
    return [jnp.where(edge, rolled[(k + 2) % 3], rolled[k]) for k in range(3)]


def from_right(tiles, steps):
    rolled = [pltpu.roll(t, 128 - steps, 1) for t in tiles]
    edge = lanes() >= 128 - steps
    return [jnp.where(edge, rolled[(k + 1) % 3], rolled[k]) for k in range(3)]


def ext_block(main, top, bottom, offset, block, k):
    cols = pl.ds(128 * k, 128)
    if block < 2:
        return top(offset + 8 * block, cols)
    if block >= BLOCKS - 2:
        return bottom(offset + 8 * (block - (BLOCKS - 2)), cols)
    return main[0, pl.ds(8 * (block - 2), 8), cols]


def halo_rows(from_odd, from_even):
    is_odd = lax.rem(lax.axis_index("row"), 2) == 1

    def top(row, cols):
        return jnp.where(is_odd, from_even[pl.ds(row, 8), cols], from_odd[pl.ds(row, 8), cols])

    def bottom(row, cols):
        return jnp.where(is_odd, from_odd[pl.ds(row, 8), cols], from_even[pl.ds(row, 8), cols])

    return top, bottom


def strip_kernel(image, stiff, later, row_o, row_e, later_o, later_e, out_o, out_e):
    top, bottom = halo_rows(row_o, row_e)
    later_top, later_bottom = halo_rows(later_o, later_e)
    is_odd = lax.rem(lax.axis_index("col"), 2) == 1
    lane = lanes()
    sources = ((image, top, bottom, 0), (stiff, top, bottom, RIM), (later, later_top, later_bottom, 0))
    for n, (main, up, down, offset) in enumerate(sources):
        left = [jnp.zeros((8, 128), jnp.float32)] * GROUP
        right = [jnp.zeros((8, 128), jnp.float32)] * GROUP
        for block in range(BLOCKS):
            g, place = divmod(block, GROUP)
            here = (lane >= 16 * g) & (lane < 16 * g + 16)
            first = ext_block(main, up, down, offset, block, 0)
            last = ext_block(main, up, down, offset, block, 1)
            first = pltpu.roll(first, 16 * g, 1) if g else first
            last = pltpu.roll(last, (16 + 16 * g) % 128, 1) if g != 7 else last
            left[place] = jnp.where(here, first, left[place])
            right[place] = jnp.where(here, last, right[place])
        for place in range(GROUP):
            rows = pl.ds(8 * (GROUP * n + place), 8)
            out_o[rows, :] = jnp.where(is_odd, right[place], left[place])
            out_e[rows, :] = jnp.where(is_odd, left[place], right[place])


def sweep(g, rhs, matrix, block):
    row = pl.multiple_of(8 * block, 8)
    here = pl.ds(row, 8)
    sums = []
    for comp in range(2):
        cur = [g[comp, k, here, :] for k in range(3)]
        up = [g[comp, k, pl.ds(row - 1, 8), :] for k in range(3)]
        down = [g[comp, k, pl.ds(row + 1, 8), :] for k in range(3)]
        left = from_left(cur, 1)
        right = from_right(cur, 1)
        sums.append([(up[k] + down[k]) + (left[k] + right[k]) for k in range(3)])
    return [
        [
            rhs[0, k, here, :] + (matrix[0, k, here, :] * sums[0][k] - matrix[1, k, here, :] * sums[1][k])
            for k in range(3)
        ],
        [
            rhs[1, k, here, :] + (matrix[2, k, here, :] * sums[1][k] - matrix[1, k, here, :] * sums[0][k])
            for k in range(3)
        ],
    ]


def clear_rims(ref, count):
    zero = jnp.zeros((8, 128), jnp.float32)
    for comp in range(count):
        for k in range(3):
            ref[comp, k, pl.ds(0, 8), :] = zero
            ref[comp, k, pl.ds(EXT - 8, 8), :] = zero


def first_kernel(
    image, stiff, later, row_o, row_e, later_o, later_e, col_o, col_e,
    tensor_out, rhs, matrix, inverse, field, sent,
    img, chg, root, prods, work,
):
    lane = lanes()
    sub = lax.broadcasted_iota(jnp.int32, (8, 128), 0)
    zero = jnp.zeros((8, 128), jnp.float32)
    s, r, c = (lax.axis_index(name) for name in AXES)
    rows, cols = lax.axis_size("row"), lax.axis_size("col")
    top, bottom = halo_rows(row_o, row_e)
    later_top, later_bottom = halo_rows(later_o, later_e)
    is_odd = lax.rem(c, 2) == 1

    for k in range(3):
        img[k, pl.ds(0, 8), :] = zero
        img[k, pl.ds(EXT + 8, 8), :] = zero

    def beside(n, block):
        g, place = divmod(block, GROUP)
        at = pl.ds(8 * (GROUP * n + place), 8)
        a, b = col_o[at, :], col_e[at, :]
        right = jnp.where(is_odd, a, b)
        left = jnp.where(is_odd, b, a)
        right = pltpu.roll(right, (128 - 16 * g) % 128, 1) if g else right
        left = pltpu.roll(left, (112 - 16 * g) % 128, 1) if g != 7 else left
        return jnp.where(lane < 16, right, jnp.where(lane >= 112, left, zero))

    for block in range(BLOCKS):
        at = pl.ds(8 * block, 8)
        for k in range(3):
            if k < 2:
                a = ext_block(image, top, bottom, 0, block, k)
                b = ext_block(later, later_top, later_bottom, 0, block, k)
                q = ext_block(stiff, top, bottom, RIM, block, k)
            else:
                a, q, b = beside(0, block), beside(1, block), beside(2, block)
            img[k, pl.ds(8 * block + 8, 8), :] = a
            chg[k, at, :] = b - a
            root[k, at, :] = jnp.sqrt(q)

    low = jnp.where(r == 0, RIM, 0)
    high = jnp.where(r == rows - 1, RIM + TILE, EXT)
    col_ok = ((lane < 16) & (c < cols - 1)) | ((lane >= 112) & (c > 0))

    def gradient(block, carry):
        row = pl.multiple_of(8 * block, 8)
        at = pl.ds(row, 8)
        here = sub + row
        row_ok = (here >= low) & (here < high)
        cur = [img[k, pl.ds(row + 8, 8), :] for k in range(3)]
        left = from_left(cur, 1)
        right = from_right(cur, 1)
        for k in range(3):
            ok = row_ok & col_ok if k == 2 else row_ok
            gx = jnp.where(ok, (right[k] - left[k]) * 0.5, 0.0)
            gy = jnp.where(ok, (img[k, pl.ds(row + 9, 8), :] - img[k, pl.ds(row + 7, 8), :]) * 0.5, 0.0)
            d = chg[k, at, :]
            prods[0, k, at, :] = gx * gx
            prods[1, k, at, :] = gx * gy
            prods[2, k, at, :] = gy * gy
            prods[3, k, at, :] = gx * d
            prods[4, k, at, :] = gy * d
        return carry

    lax.fori_loop(0, BLOCKS, gradient, 0)

    scale = jnp.where(s < lax.axis_size("sec") - 1, 1.0 / float((2 * RADIUS + 1) ** 2), 0.0)
    clear_rims(field, 2)
    clear_rims(work, 2)

    def system(block, store):
        row = pl.multiple_of(8 * block, 8)
        at = pl.ds(row, 8)
        tensor = []
        for p in range(5):
            tall = []
            for k in range(3):
                terms = [prods[p, k, pl.ds(row + d, 8), :] for d in range(-RADIUS, RADIUS + 1)]
                while len(terms) > 1:
                    terms = [sum(terms[i : i + 2]) for i in range(0, len(terms), 2)]
                tall.append(terms[0])
            two = [a + b for a, b in zip(tall, from_right(tall, 1))]
            four = [a + b for a, b in zip(two, from_right(two, 2))]
            eight = [a + b for a, b in zip(four, from_right(four, 4))]
            whole = [a + b for a, b in zip(from_left(eight, 4), from_right(tall, 4))]
            tensor.append([w * scale for w in whole])
        if store:
            for p in range(5):
                for k in range(2):
                    tensor_out[p, 0, pl.ds(pl.multiple_of(row - RIM, 8), 8), pl.ds(128 * k, 128)] = tensor[p][k]
        cur = [root[k, at, :] for k in range(3)]
        left = from_left(cur, 1)
        right = from_right(cur, 1)
        for k in range(3):
            q = cur[k]
            around = (root[k, pl.ds(row - 1, 8), :] + root[k, pl.ds(row + 1, 8), :]) + (left[k] + right[k])
            diag = q * around + 2.0 * COUPLING
            xx, xy, yy, xt, yt = (tensor[p][k] for p in range(5))
            first, second = xx + diag, yy + diag
            over = q / (first * second - xy * xy)
            a, b, d = second * over, xy * over, first * over
            rx = b * yt - a * xt
            ry = b * xt - d * yt
            rhs[0, k, at, :] = rx
            rhs[1, k, at, :] = ry
            work[0, k, at, :] = rx
            work[1, k, at, :] = ry
            matrix[0, k, at, :] = a * q
            matrix[1, k, at, :] = b * q
            matrix[2, k, at, :] = d * q
            inverse[k, at, :] = jnp.where(q > 0.0, 1.0 / q, 0.0)

    def stored(block, carry):
        system(block, True)
        return carry

    system(1, False)
    lax.fori_loop(2, BLOCKS - 2, stored, 0)
    system(BLOCKS - 2, False)

    def step(src, dst):
        def body(block, carry):
            new = sweep(src, rhs, matrix, block)
            at = pl.ds(pl.multiple_of(8 * block, 8), 8)
            for comp in range(2):
                for k in range(3):
                    dst[comp, k, at, :] = new[comp][k]
            return carry

        lax.fori_loop(1, BLOCKS - 1, body, 0)

    step(work, field)
    step(field, work)

    def last(block, carry):
        new = sweep(work, rhs, matrix, block)
        at = pl.ds(pl.multiple_of(8 * block, 8), 8)
        for comp in range(2):
            for k in range(3):
                field[comp, k, at, :] = new[comp][k]
            for k in range(2):
                base = (2 * comp + k) * 8 * INNER
                sent[pl.ds(pl.multiple_of(base + 8 * block - 8, 8), 8), :] = new[comp][k] * inverse[k, at, :]
        return carry

    lax.fori_loop(1, BLOCKS - 1, last, 0)

    for comp in range(2):
        strip = [zero] * GROUP
        for block in range(INNER):
            g, place = divmod(block, GROUP)
            at = pl.ds(8 * block + 8, 8)
            tile = field[comp, 2, at, :] * inverse[2, at, :]
            tile = pltpu.roll(tile, FIELD_RIM + 16 * g, 1)
            strip[place] = jnp.where((lane >= 16 * g) & (lane < 16 * g + 16), tile, strip[place])
        for place in range(GROUP):
            sent[pl.ds(32 * INNER + 8 * (GROUP * comp + place), 8), :] = strip[place]


def second_kernel(rhs, matrix, inverse, field, far, near, out, moved, work_a, work_b, strips):
    lane = lanes()
    zero = jnp.zeros((8, 128), jnp.float32)
    clear_rims(work_a, 2)
    clear_rims(work_b, 2)
    for comp in range(2):
        for block in range(INNER):
            g, place = divmod(block, GROUP)
            at = pl.ds(32 * INNER + 8 * (GROUP * comp + place), 8)
            tile = pltpu.roll(far[at, :] + near[at, :], 128 - FIELD_RIM - 16 * g, 1)
            strips[comp, pl.ds(8 * block, 8), :] = jnp.where((lane < FIELD_RIM) | (lane >= 128 - FIELD_RIM), tile, zero)

    def right_side(block, carry):
        at = pl.ds(pl.multiple_of(8 * block, 8), 8)
        for k in range(3):
            pair = []
            for comp in range(2):
                if k < 2:
                    base = (2 * comp + k) * 8 * INNER
                    rows = pl.ds(pl.multiple_of(base + 8 * block - 8, 8), 8)
                    value = far[rows, :] + near[rows, :]
                else:
                    value = strips[comp, pl.ds(pl.multiple_of(8 * block - 8, 8), 8), :]
                pair.append(value * (inverse[k, at, :] * COUPLING))
            a, b, d = (matrix[i, k, at, :] for i in range(3))
            moved[0, k, at, :] = rhs[0, k, at, :] + (a * pair[0] - b * pair[1])
            moved[1, k, at, :] = rhs[1, k, at, :] + (d * pair[1] - b * pair[0])
        return carry

    lax.fori_loop(1, BLOCKS - 1, right_side, 0)

    def step(src, dst):
        def body(block, carry):
            new = sweep(src, moved, matrix, block)
            at = pl.ds(pl.multiple_of(8 * block, 8), 8)
            for comp in range(2):
                for k in range(3):
                    dst[comp, k, at, :] = new[comp][k]
            return carry

        lax.fori_loop(1, BLOCKS - 1, body, 0)

    step(field, work_a)
    step(work_a, work_b)
    step(work_b, work_a)

    def last(block, carry):
        new = sweep(work_a, moved, matrix, block)
        at = pl.ds(pl.multiple_of(8 * block, 8), 8)
        for comp in range(2):
            for k in range(2):
                out[comp, 0, pl.ds(pl.multiple_of(8 * block - RIM, 8), 8), pl.ds(128 * k, 128)] = (
                    new[comp][k] * inverse[k, at, :]
                )
        return carry

    lax.fori_loop(2, BLOCKS - 2, last, 0)


def f32(*shape):
    return jax.ShapeDtypeStruct(shape, jnp.float32)


def vmem(*shape):
    return pltpu.VMEM(shape, jnp.float32)


def local(images, stiffness):
    row_odd = lax.rem(lax.axis_index("row"), 2) == 1
    tops = jnp.concatenate([images[0, :RIM], stiffness[0, :RIM]], axis=0)
    bottoms = jnp.concatenate([images[0, TILE - RIM :], stiffness[0, TILE - RIM :]], axis=0)
    to_o = jnp.where(row_odd, bottoms, tops)
    to_e = jnp.where(row_odd, tops, bottoms)
    later = send(images, sec_of=earlier)
    later_o = send(to_o, sec_of=earlier, row_of=odd)
    later_e = send(to_e, sec_of=earlier, row_of=even)
    row_o = send(to_o, row_of=odd)
    row_e = send(to_e, row_of=even)

    pieces = (images, stiffness, later, row_o, row_e, later_o, later_e)
    strip = f32(3 * GROUP * 8, 128)
    strip_o, strip_e = pl.pallas_call(strip_kernel, out_shape=(strip, strip))(*pieces)
    col_o = send(strip_o, col_of=odd)
    col_e = send(strip_e, col_of=even)

    grid = (3, EXT, 128)
    sent_rows = 32 * INNER + 16 * GROUP
    tensor, rhs, matrix, inverse, field, sent = pl.pallas_call(
        first_kernel,
        out_shape=(f32(5, 1, TILE, TILE), f32(2, *grid), f32(3, *grid), f32(*grid), f32(2, *grid), f32(sent_rows, 128)),
        scratch_shapes=[vmem(3, EXT + 16, 128), vmem(*grid), vmem(*grid), vmem(5, *grid), vmem(2, *grid)],
        compiler_params=pltpu.CompilerParams(vmem_limit_bytes=40 << 20),
    )(*pieces, col_o, col_e)

    far = send(sent, sec_of=odd)
    near = send(sent, sec_of=even)
    field = pl.pallas_call(
        second_kernel,
        out_shape=f32(2, 1, TILE, TILE),
        scratch_shapes=[vmem(2, *grid), vmem(2, *grid), vmem(2, *grid), vmem(2, 8 * INNER, 128)],
        compiler_params=pltpu.CompilerParams(vmem_limit_bytes=40 << 20),
    )(rhs, matrix, inverse, field, far, near)
    return tensor, field


def solution(mesh):
    in_specs = (P("sec", "row", "col"), P("sec", "row", "col"))
    out_specs = (P(None, "sec", "row", "col"), P(None, "sec", "row", "col"))
    return jax.shard_map(local, mesh=mesh, in_specs=in_specs, out_specs=out_specs, check_vma=False)
```

```python
import jax
import jax.numpy as jnp
from jax import lax
from jax.experimental import pallas as pl
from jax.experimental.pallas import tpu as pltpu
from jax.sharding import PartitionSpec as P

RADIUS = 4
COUPLING = 0.25
AXES = ("sec", "row", "col")

TILE = 256
RIM = 16
EXT = TILE + 2 * RIM
BLOCKS = EXT // 8
INNER = BLOCKS - 2
GROUP = 5
FIELD_RIM = 8
STRIP = GROUP * 8


def even(i, count):
    j = i ^ 1
    return j if j < count else None


def odd(i, count):
    j = ((i + 1) ^ 1) - 1
    return j if 0 <= j < count else None


def same(i, count):
    return i


def pairs(sec_of, row_of, col_of):
    secs, rows, cols = (lax.axis_size(name) for name in AXES)
    found = []
    for s in range(secs):
        for r in range(rows):
            for c in range(cols):
                to = (sec_of(s, secs), row_of(r, rows), col_of(c, cols))
                if None not in to:
                    found.append(((s * rows + r) * cols + c, (to[0] * rows + to[1]) * cols + to[2]))
    return found


def send(value, sec_of=same, row_of=same, col_of=same):
    return lax.ppermute(value, AXES, pairs(sec_of, row_of, col_of))


def earlier(s, count):
    return s - 1 if s > 0 else None


def lanes():
    return lax.broadcasted_iota(jnp.int32, (8, 128), 1)


def from_left(tiles, steps):
    rolled = [pltpu.roll(t, steps, 1) for t in tiles]
    edge = lanes() < steps
    return [jnp.where(edge, rolled[(k + 2) % 3], rolled[k]) for k in range(3)]


def from_right(tiles, steps):
    rolled = [pltpu.roll(t, 128 - steps, 1) for t in tiles]
    edge = lanes() >= 128 - steps
    return [jnp.where(edge, rolled[(k + 1) % 3], rolled[k]) for k in range(3)]


def ext_block(main, top, bottom, block, k):
    cols = pl.ds(128 * k, 128)
    if block < 2:
        return top(8 * block, cols)
    if block >= BLOCKS - 2:
        return bottom(8 * (block - (BLOCKS - 2)), cols)
    return main(8 * (block - 2), cols)


def reader(ref, offset=0):
    return lambda row, cols: ref[pl.ds(offset + row, 8), cols]


def choose(flag, a, b):
    return lambda row, cols: jnp.where(flag, a(row, cols), b(row, cols))


def is_odd(axis):
    return lax.rem(lax.axis_index(axis), 2) == 1


def prepare_kernel(image, stiff, img, root, out_o, out_e):
    flag = is_odd("row")
    for n in range(TILE // 8):
        rows = pl.ds(8 * n, 8)
        img[rows, :] = image[0, rows, :]
        root[rows, :] = jnp.sqrt(stiff[0, rows, :])
    for m, ref in enumerate((img, root)):
        for n in range(RIM // 8):
            first = ref[pl.ds(8 * n, 8), :]
            last = ref[pl.ds(TILE - RIM + 8 * n, 8), :]
            rows = pl.ds(RIM * m + 8 * n, 8)
            out_o[rows, :] = jnp.where(flag, last, first)
            out_e[rows, :] = jnp.where(flag, first, last)


def strip_kernel(img, root, row_o, row_e, out_o, out_e):
    row_flag, col_flag = is_odd("row"), is_odd("col")
    lane = lanes()
    for n, main in enumerate((img, root)):
        from_o, from_e = reader(row_o, RIM * n), reader(row_e, RIM * n)
        top, bottom = choose(row_flag, from_e, from_o), choose(row_flag, from_o, from_e)
        left = [jnp.zeros((8, 128), jnp.float32)] * GROUP
        right = [jnp.zeros((8, 128), jnp.float32)] * GROUP
        for block in range(BLOCKS):
            g, place = divmod(block, GROUP)
            here = (lane >= 16 * g) & (lane < 16 * g + 16)
            first = ext_block(reader(main), top, bottom, block, 0)
            last = ext_block(reader(main), top, bottom, block, 1)
            first = pltpu.roll(first, 16 * g, 1) if g else first
            last = pltpu.roll(last, (16 + 16 * g) % 128, 1) if g != 7 else last
            left[place] = jnp.where(here, first, left[place])
            right[place] = jnp.where(here, last, right[place])
        for place in range(GROUP):
            rows = pl.ds(STRIP * n + 8 * place, 8)
            out_o[rows, :] = jnp.where(col_flag, right[place], left[place])
            out_e[rows, :] = jnp.where(col_flag, left[place], right[place])


def rims_kernel(row_o, row_e, col_o, col_e, out):
    for m, ref in enumerate((row_o, row_e)):
        for k in range(2):
            for n in range(RIM // 8):
                out[pl.ds(RIM * (2 * m + k) + 8 * n, 8), :] = ref[pl.ds(8 * n, 8), pl.ds(128 * k, 128)]
    for m, ref in enumerate((col_o, col_e)):
        for n in range(GROUP):
            out[pl.ds(4 * RIM + STRIP * m + 8 * n, 8), :] = ref[pl.ds(8 * n, 8), :]


def side_block(from_o, from_e, flag, block):
    lane = lanes()
    g, place = divmod(block, GROUP)
    cols = pl.ds(0, 128)
    a, b = from_o(8 * place, cols), from_e(8 * place, cols)
    right = jnp.where(flag, a, b)
    left = jnp.where(flag, b, a)
    right = pltpu.roll(right, 128 - 16 * g, 1) if g else right
    left = pltpu.roll(left, (112 - 16 * g) % 128, 1) if g != 7 else left
    return jnp.where(lane < 16, right, jnp.where(lane >= 112, left, 0.0))


def window(tiles):
    three = [a + (b + c) for a, b, c in zip(tiles, from_left(tiles, 1), from_right(tiles, 1))]
    return [a + (b + c) for a, b, c in zip(three, from_left(three, 3), from_right(three, 3))]


def tall(ref, p, k, row):
    terms = [ref[p, k, pl.ds(row + d, 8), :] for d in range(-RADIUS, RADIUS + 1)]
    while len(terms) > 1:
        terms = [sum(terms[i : i + 2]) for i in range(0, len(terms), 2)]
    return terms[0]


def mean_scale():
    keep = lax.axis_index("sec") < lax.axis_size("sec") - 1
    return jnp.where(keep, 1.0 / float((2 * RADIUS + 1) ** 2), 0.0)


def matrix_kernel(img, root, row_o, row_e, col_o, col_e, ext, gx_out, gy_out, matrix, inverse, tensor, wide, sums):
    lane = lanes()
    sub = lax.broadcasted_iota(jnp.int32, (8, 128), 0)
    zero = jnp.zeros((8, 128), jnp.float32)
    row_flag, col_flag = is_odd("row"), is_odd("col")
    r, c = lax.axis_index("row"), lax.axis_index("col")
    rows, cols = lax.axis_size("row"), lax.axis_size("col")

    for k in range(3):
        ext[k, pl.ds(0, 8), :] = zero
        ext[k, pl.ds(EXT + 8, 8), :] = zero
    for n, (main, dst, shift) in enumerate(((img, ext, 8), (root, wide, 0))):
        from_o, from_e = reader(row_o, RIM * n), reader(row_e, RIM * n)
        top, bottom = choose(row_flag, from_e, from_o), choose(row_flag, from_o, from_e)
        side_o, side_e = reader(col_o, STRIP * n), reader(col_e, STRIP * n)
        for block in range(BLOCKS):
            at = pl.ds(8 * block + shift, 8)
            for k in range(2):
                dst[k, at, :] = ext_block(reader(main), top, bottom, block, k)
            dst[2, at, :] = side_block(side_o, side_e, col_flag, block)

    low = jnp.where(r == 0, RIM, 0)
    high = jnp.where(r == rows - 1, RIM + TILE, EXT)
    col_ok = ((lane < 16) & (c < cols - 1)) | ((lane >= 112) & (c > 0))

    def gradient(block, carry):
        row = pl.multiple_of(8 * block, 8)
        at = pl.ds(row, 8)
        here = sub + row
        row_ok = (here >= low) & (here < high)
        cur = [ext[k, pl.ds(row + 8, 8), :] for k in range(3)]
        left = from_left(cur, 1)
        right = from_right(cur, 1)
        gx, gy = [], []
        for k in range(3):
            ok = row_ok & col_ok if k == 2 else row_ok
            gx.append(jnp.where(ok, (right[k] - left[k]) * 0.5, 0.0))
            gy.append(jnp.where(ok, (ext[k, pl.ds(row + 9, 8), :] - ext[k, pl.ds(row + 7, 8), :]) * 0.5, 0.0))
            gx_out[k, at, :] = gx[k]
            gy_out[k, at, :] = gy[k]
        for p, (a, b) in enumerate(((gx, gx), (gx, gy), (gy, gy))):
            total = window([u * v for u, v in zip(a, b)])
            for k in range(3):
                sums[p, k, at, :] = total[k]
        return carry

    lax.fori_loop(0, BLOCKS, gradient, 0, unroll=6)
    scale = mean_scale()

    def system(block, carry):
        row = pl.multiple_of(8 * block, 8)
        at = pl.ds(row, 8)
        cur = [wide[k, at, :] for k in range(3)]
        left = from_left(cur, 1)
        right = from_right(cur, 1)
        for k in range(3):
            xx, xy, yy = (tall(sums, p, k, row) * scale for p in range(3))
            if k < 2:
                for p, value in enumerate((xx, xy, yy)):
                    tensor[p, at, pl.ds(128 * k, 128)] = value
            q = cur[k]
            around = (wide[k, pl.ds(row - 1, 8), :] + wide[k, pl.ds(row + 1, 8), :]) + (left[k] + right[k])
            diag = q * around + 2.0 * COUPLING
            first, second = xx + diag, yy + diag
            over = (q * q) / (first * second - xy * xy)
            matrix[0, k, at, :] = second * over
            matrix[1, k, at, :] = xy * over
            matrix[2, k, at, :] = first * over
            inverse[k, at, :] = jnp.where(q > 0.0, 1.0 / q, 0.0)
        return carry

    lax.fori_loop(1, BLOCKS - 1, system, 0, unroll=2)


def clear_rims(ref):
    zero = jnp.zeros((8, 128), jnp.float32)
    for comp in range(2):
        for k in range(3):
            ref[comp, k, pl.ds(0, 8), :] = zero
            ref[comp, k, pl.ds(EXT - 8, 8), :] = zero


def sweep(g, rhs, matrix, block):
    row = pl.multiple_of(8 * block, 8)
    here = pl.ds(row, 8)
    sums = []
    for comp in range(2):
        cur = [g[comp, k, here, :] for k in range(3)]
        up = [g[comp, k, pl.ds(row - 1, 8), :] for k in range(3)]
        down = [g[comp, k, pl.ds(row + 1, 8), :] for k in range(3)]
        left = from_left(cur, 1)
        right = from_right(cur, 1)
        sums.append([(up[k] + down[k]) + (left[k] + right[k]) for k in range(3)])
    first, second = [], []
    for k in range(3):
        a, b, d = (matrix[i, k, here, :] for i in range(3))
        first.append(rhs[0, k, here, :] + (a * sums[0][k] - b * sums[1][k]))
        second.append(rhs[1, k, here, :] + (d * sums[1][k] - b * sums[0][k]))
    return first, second


def step(src, dst, rhs, matrix):
    def body(block, carry):
        new = sweep(src, rhs, matrix, block)
        at = pl.ds(pl.multiple_of(8 * block, 8), 8)
        for comp in range(2):
            for k in range(3):
                dst[comp, k, at, :] = new[comp][k]
        return carry

    lax.fori_loop(1, BLOCKS - 1, body, 0, unroll=17)


def first_kernel(
    ext, gx, gy, matrix, inverse, known, later, rims,
    tensor, rhs, field, sent,
    chg, sums, work, fresh, sems,
):
    lane = lanes()
    zero = jnp.zeros((8, 128), jnp.float32)
    row_flag, col_flag = is_odd("row"), is_odd("col")
    inner = pl.ds(RIM, TILE)
    copies = [pltpu.make_async_copy(known.at[:, inner], tensor.at[pl.ds(0, 3), 0], sems.at[0])]
    copies[0].start()

    def rim_rows(base):
        return lambda row, cols: rims[pl.ds(base + RIM * (cols.start // 128) + row, 8), :]

    from_o, from_e = rim_rows(0), rim_rows(2 * RIM)
    top, bottom = choose(row_flag, from_e, from_o), choose(row_flag, from_o, from_e)
    side_o, side_e = reader(rims, 4 * RIM), reader(rims, 4 * RIM + STRIP)
    main = lambda row, cols: later[0, pl.ds(row, 8), cols]
    for block in range(BLOCKS):
        at = pl.ds(8 * block, 8)
        old = pl.ds(8 * block + 8, 8)
        for k in range(2):
            chg[k, at, :] = ext_block(main, top, bottom, block, k) - ext[k, old, :]
        chg[2, at, :] = side_block(side_o, side_e, col_flag, block) - ext[2, old, :]

    def products(block, carry):
        at = pl.ds(pl.multiple_of(8 * block, 8), 8)
        for p, grad in enumerate((gx, gy)):
            total = window([grad[k, at, :] * chg[k, at, :] for k in range(3)])
            for k in range(3):
                sums[p, k, at, :] = total[k]
        return carry

    lax.fori_loop(0, BLOCKS, products, 0, unroll=6)
    scale = mean_scale()
    clear_rims(field)
    clear_rims(work)

    def right_side(block, carry):
        row = pl.multiple_of(8 * block, 8)
        at = pl.ds(row, 8)
        for k in range(3):
            xt, yt = (tall(sums, p, k, row) * scale for p in range(2))
            if k < 2:
                fresh[0, at, pl.ds(128 * k, 128)] = xt
                fresh[1, at, pl.ds(128 * k, 128)] = yt
            a, b, d = (matrix[i, k, at, :] for i in range(3))
            inv = inverse[k, at, :]
            rx = (b * yt - a * xt) * inv
            ry = (b * xt - d * yt) * inv
            rhs[0, k, at, :] = rx
            rhs[1, k, at, :] = ry
            work[0, k, at, :] = rx
            work[1, k, at, :] = ry
        return carry

    lax.fori_loop(1, BLOCKS - 1, right_side, 0, unroll=2)
    copies.append(pltpu.make_async_copy(fresh.at[:, inner], tensor.at[pl.ds(3, 2), 0], sems.at[1]))
    copies[1].start()

    step(work, field, rhs, matrix)
    step(field, work, rhs, matrix)

    def last(block, carry):
        new = sweep(work, rhs, matrix, block)
        at = pl.ds(pl.multiple_of(8 * block, 8), 8)
        for comp in range(2):
            for k in range(3):
                field[comp, k, at, :] = new[comp][k]
            for k in range(2):
                base = (2 * comp + k) * 8 * INNER
                sent[pl.ds(pl.multiple_of(base + 8 * block - 8, 8), 8), :] = new[comp][k] * inverse[k, at, :]
        return carry

    lax.fori_loop(1, BLOCKS - 1, last, 0, unroll=17)

    for comp in range(2):
        strip = [zero] * GROUP
        for block in range(INNER):
            g, place = divmod(block, GROUP)
            at = pl.ds(8 * block + 8, 8)
            tile = field[comp, 2, at, :] * inverse[2, at, :]
            tile = pltpu.roll(tile, FIELD_RIM + 16 * g, 1)
            strip[place] = jnp.where((lane >= 16 * g) & (lane < 16 * g + 16), tile, strip[place])
        for place in range(GROUP):
            sent[pl.ds(32 * INNER + STRIP * comp + 8 * place, 8), :] = strip[place]
    for copy in copies:
        copy.wait()


def second_kernel(rhs, matrix, inverse, field, far, near, out, moved, work_a, work_b, strips):
    lane = lanes()
    clear_rims(work_a)
    clear_rims(work_b)
    for comp in range(2):
        for block in range(INNER):
            g, place = divmod(block, GROUP)
            at = pl.ds(32 * INNER + STRIP * comp + 8 * place, 8)
            tile = pltpu.roll(far[at, :] + near[at, :], 128 - FIELD_RIM - 16 * g, 1)
            strips[comp, pl.ds(8 * block, 8), :] = jnp.where((lane < FIELD_RIM) | (lane >= 128 - FIELD_RIM), tile, 0.0)

    def right_side(block, carry):
        at = pl.ds(pl.multiple_of(8 * block, 8), 8)
        for k in range(3):
            pair = []
            for comp in range(2):
                if k < 2:
                    base = (2 * comp + k) * 8 * INNER
                    rows = pl.ds(pl.multiple_of(base + 8 * block - 8, 8), 8)
                    value = far[rows, :] + near[rows, :]
                else:
                    value = strips[comp, pl.ds(pl.multiple_of(8 * block - 8, 8), 8), :]
                pair.append(value * (inverse[k, at, :] * COUPLING))
            a, b, d = (matrix[i, k, at, :] for i in range(3))
            moved[0, k, at, :] = rhs[0, k, at, :] + (a * pair[0] - b * pair[1])
            moved[1, k, at, :] = rhs[1, k, at, :] + (d * pair[1] - b * pair[0])
        return carry

    lax.fori_loop(1, BLOCKS - 1, right_side, 0, unroll=17)

    step(field, work_a, moved, matrix)
    step(work_a, work_b, moved, matrix)
    step(work_b, work_a, moved, matrix)

    def last(block, carry):
        new = sweep(work_a, moved, matrix, block)
        at = pl.ds(pl.multiple_of(8 * block, 8), 8)
        for comp in range(2):
            for k in range(2):
                out[comp, 0, pl.ds(pl.multiple_of(8 * block - RIM, 8), 8), pl.ds(128 * k, 128)] = (
                    new[comp][k] * inverse[k, at, :]
                )
        return carry

    lax.fori_loop(2, BLOCKS - 2, last, 0, unroll=16)


def f32(*shape):
    return jax.ShapeDtypeStruct(shape, jnp.float32)


def vmem(*shape):
    return pltpu.VMEM(shape, jnp.float32)


def call(kernel, out_shape, args, mib=6, us=0, **rest):
    return pl.pallas_call(
        kernel,
        out_shape=out_shape,
        compiler_params=pltpu.CompilerParams(vmem_limit_bytes=mib << 20),
        cost_estimate=pl.CostEstimate(flops=us * 1000000, bytes_accessed=us * 3000000, transcendentals=0),
        **rest,
    )(*args)


def local(images, stiffness):
    grid = (3, EXT, 128)
    edge, strip = f32(2 * RIM, TILE), f32(2 * STRIP, 128)
    later = send(images, sec_of=earlier)
    img, root, to_o, to_e = call(prepare_kernel, (f32(TILE, TILE),) * 2 + (edge,) * 2, (images, stiffness), us=1)
    row_o = send(to_o, row_of=odd)
    row_e = send(to_e, row_of=even)

    strip_o, strip_e = call(strip_kernel, (strip, strip), (img, root, row_o, row_e))
    col_o = send(strip_o, col_of=odd)
    col_e = send(strip_e, col_of=even)

    rims = call(rims_kernel, f32(4 * RIM + 2 * STRIP, 128), (row_o, row_e, col_o, col_e))
    rims = send(rims, sec_of=earlier)
    ext, gx, gy, matrix, inverse, known = call(
        matrix_kernel,
        (f32(3, EXT + 16, 128), f32(*grid), f32(*grid), f32(3, *grid), f32(*grid), f32(3, EXT, TILE)),
        (img, root, row_o, row_e, col_o, col_e),
        mib=16,
        us=4,
        scratch_shapes=[vmem(*grid), vmem(3, *grid)],
    )
    sent_rows = 32 * INNER + 2 * STRIP
    everywhere = [pl.BlockSpec(memory_space=pltpu.VMEM)] * 3
    tensor, rhs, field, sent = call(
        first_kernel,
        (f32(5, 1, TILE, TILE), f32(2, *grid), f32(2, *grid), f32(sent_rows, 128)),
        (ext, gx, gy, matrix, inverse, known, later, rims),
        mib=20,
        us=5,
        out_specs=[pl.BlockSpec(memory_space=pl.ANY)] + everywhere,
        scratch_shapes=[vmem(*grid), vmem(2, *grid), vmem(2, *grid), vmem(2, EXT, TILE), pltpu.SemaphoreType.DMA((2,))],
    )

    far = send(sent, sec_of=odd)
    near = send(sent, sec_of=even)
    field = call(
        second_kernel,
        f32(2, 1, TILE, TILE),
        (rhs, matrix, inverse, field, far, near),
        mib=20,
        us=4,
        scratch_shapes=[vmem(2, *grid), vmem(2, *grid), vmem(2, *grid), vmem(2, 8 * INNER, 128)],
    )
    return tensor, field


def solution(mesh):
    in_specs = (P("sec", "row", "col"), P("sec", "row", "col"))
    out_specs = (P(None, "sec", "row", "col"), P(None, "sec", "row", "col"))
    return jax.shard_map(local, mesh=mesh, in_specs=in_specs, out_specs=out_specs, check_vma=False)
```

```python
import jax
import jax.numpy as jnp
from jax import lax
from jax.experimental import pallas as pl
from jax.experimental.pallas import tpu as pltpu
from jax.sharding import PartitionSpec as P

RADIUS = 4
COUPLING = 0.25
AXES = ("sec", "row", "col")

TILE = 256
RIM = 16
EXT = TILE + 2 * RIM
BLOCKS = EXT // 8
INNER = BLOCKS - 2
GROUP = 5
FIELD_RIM = 8
CUTS = 4
STRIP = GROUP * 8
RIMS = 4 * RIM + 2 * STRIP


def sizes():
    return [lax.axis_size(name) for name in AXES]


def even(i):
    return i ^ 1


def odd(i):
    return ((i + 1) ^ 1) - 1


def send(value, move):
    secs, rows, cols = sizes()
    found = []
    for s in range(secs):
        for r in range(rows):
            for c in range(cols):
                to = move(s, r, c, secs, rows, cols)
                found.append(((s * rows + r) * cols + c, (to[0] * rows + to[1]) * cols + to[2]))
    return lax.ppermute(value, AXES, found)


def row_even(s, r, c, secs, rows, cols):
    return s, even(r), c


def row_odd(s, r, c, secs, rows, cols):
    if 0 < r < rows - 1:
        return s, odd(r), c
    return s, r, even(c)


def col_even(s, r, c, secs, rows, cols):
    return s, r, even(c)


def col_odd(s, r, c, secs, rows, cols):
    if 0 < c < cols - 1:
        return s, r, odd(c)
    return s, even(r), c


def sec_even(s, r, c, secs, rows, cols):
    return even(s), r, c


def sec_odd(s, r, c, secs, rows, cols):
    if 0 < s < secs - 1:
        return odd(s), r, c
    return s, even(r), c


def lanes():
    return lax.broadcasted_iota(jnp.int32, (8, 128), 1)


def from_left(tiles, steps):
    rolled = [pltpu.roll(t, steps, 1) for t in tiles]
    edge = lanes() < steps
    return [jnp.where(edge, rolled[(k + 2) % 3], rolled[k]) for k in range(3)]


def from_right(tiles, steps):
    rolled = [pltpu.roll(t, 128 - steps, 1) for t in tiles]
    edge = lanes() >= 128 - steps
    return [jnp.where(edge, rolled[(k + 1) % 3], rolled[k]) for k in range(3)]


def ext_block(main, top, bottom, block, k):
    cols = pl.ds(128 * k, 128)
    if block < 2:
        return top(8 * block, cols)
    if block >= BLOCKS - 2:
        return bottom(8 * (block - (BLOCKS - 2)), cols)
    return main(8 * (block - 2), cols)


def reader(ref, offset=0):
    return lambda row, cols: ref[pl.ds(offset + row, 8), cols]


def tile_of(ref):
    return lambda row, cols: ref[0, pl.ds(row, 8), cols]


def is_odd(axis):
    return lax.rem(lax.axis_index(axis), 2) == 1


def row_halo(from_o, from_e):
    flag = is_odd("row")
    r = lax.axis_index("row")
    above, below = r > 0, r < lax.axis_size("row") - 1

    def top(row, cols):
        return jnp.where(above, jnp.where(flag, from_e(row, cols), from_o(row, cols)), 0.0)

    def bottom(row, cols):
        return jnp.where(below, jnp.where(flag, from_o(row, cols), from_e(row, cols)), 0.0)

    return top, bottom


def prepare_kernel(image, stiff, img, stf, out_o, out_e, sems):
    flag = is_odd("row")
    copies = []
    for n in range(CUTS):
        at = pl.ds(TILE // CUTS * n, TILE // CUTS)
        copies.append(pltpu.make_async_copy(image.at[0, at], img.at[0, at], sems.at[0, n]))
        copies.append(pltpu.make_async_copy(stiff.at[0, at], stf.at[0, at], sems.at[1, n]))
    for copy in copies:
        copy.start()
    for copy in copies:
        copy.wait()
    for m, ref in enumerate((img, stf)):
        for n in range(RIM // 8):
            rows = pl.ds(RIM * m + 8 * n, 8)
            a, b = ref[0, pl.ds(8 * n, 8), :], ref[0, pl.ds(TILE - RIM + 8 * n, 8), :]
            out_o[rows, :] = jnp.where(flag, b, a)
            out_e[rows, :] = jnp.where(flag, a, b)


def strip_kernel(image, stiff, row_o, row_e, out_o, out_e):
    col_flag = is_odd("col")
    lane = lanes()
    for n, main in enumerate((image, stiff)):
        top, bottom = row_halo(reader(row_o, RIM * n), reader(row_e, RIM * n))
        left = [jnp.zeros((8, 128), jnp.float32)] * GROUP
        right = [jnp.zeros((8, 128), jnp.float32)] * GROUP
        for block in range(BLOCKS):
            g, place = divmod(block, GROUP)
            here = (lane >= 16 * g) & (lane < 16 * g + 16)
            first = ext_block(tile_of(main), top, bottom, block, 0)
            last = ext_block(tile_of(main), top, bottom, block, 1)
            first = pltpu.roll(first, 16 * g, 1) if g else first
            last = pltpu.roll(last, (16 + 16 * g) % 128, 1) if g != 7 else last
            left[place] = jnp.where(here, first, left[place])
            right[place] = jnp.where(here, last, right[place])
        for place in range(GROUP):
            rows = pl.ds(STRIP * n + 8 * place, 8)
            out_o[rows, :] = jnp.where(col_flag, right[place], left[place])
            out_e[rows, :] = jnp.where(col_flag, left[place], right[place])


def section_kernel(image, row_o, row_e, col_o, col_e, out):
    for k in range(2):
        for n in range(TILE // 8):
            out[pl.ds(RIMS + TILE * k + 8 * n, 8), :] = image[0, pl.ds(8 * n, 8), pl.ds(128 * k, 128)]
    for m, ref in enumerate((row_o, row_e)):
        for k in range(2):
            for n in range(RIM // 8):
                out[pl.ds(RIM * (2 * m + k) + 8 * n, 8), :] = ref[pl.ds(8 * n, 8), pl.ds(128 * k, 128)]
    for m, ref in enumerate((col_o, col_e)):
        for n in range(GROUP):
            out[pl.ds(4 * RIM + STRIP * m + 8 * n, 8), :] = ref[pl.ds(8 * n, 8), :]


def side_block(from_o, from_e, block):
    lane = lanes()
    c = lax.axis_index("col")
    flag = is_odd("col")
    right_ok = (lane < 16) & (c < lax.axis_size("col") - 1)
    left_ok = (lane >= 112) & (c > 0)
    g, place = divmod(block, GROUP)
    cols = pl.ds(0, 128)
    a, b = from_o(8 * place, cols), from_e(8 * place, cols)
    right = jnp.where(flag, a, b)
    left = jnp.where(flag, b, a)
    right = pltpu.roll(right, 128 - 16 * g, 1) if g else right
    left = pltpu.roll(left, (112 - 16 * g) % 128, 1) if g != 7 else left
    return jnp.where(right_ok, right, jnp.where(left_ok, left, 0.0))


def window(tiles):
    three = [a + (b + c) for a, b, c in zip(tiles, from_left(tiles, 1), from_right(tiles, 1))]
    return [a + (b + c) for a, b, c in zip(three, from_left(three, 3), from_right(three, 3))]


def tall(ref, p, k, row):
    terms = [ref[p, k, pl.ds(row + d, 8), :] for d in range(-RADIUS, RADIUS + 1)]
    while len(terms) > 1:
        terms = [sum(terms[i : i + 2]) for i in range(0, len(terms), 2)]
    return terms[0]


def mean_scale():
    keep = lax.axis_index("sec") < lax.axis_size("sec") - 1
    return jnp.where(keep, 1.0 / float((2 * RADIUS + 1) ** 2), 0.0)


def matrix_kernel(image, stiff, row_o, row_e, col_o, col_e, ext, gx_out, gy_out, matrix, inverse, tensor, wide, sums):
    lane = lanes()
    sub = lax.broadcasted_iota(jnp.int32, (8, 128), 0)
    zero = jnp.zeros((8, 128), jnp.float32)
    r, c = lax.axis_index("row"), lax.axis_index("col")
    rows, cols = lax.axis_size("row"), lax.axis_size("col")

    for k in range(3):
        ext[k, pl.ds(0, 8), :] = zero
        ext[k, pl.ds(EXT + 8, 8), :] = zero
    for n, (main, dst, shift) in enumerate(((image, ext, 8), (stiff, wide, 0))):
        top, bottom = row_halo(reader(row_o, RIM * n), reader(row_e, RIM * n))
        side_o, side_e = reader(col_o, STRIP * n), reader(col_e, STRIP * n)
        for block in range(BLOCKS):
            at = pl.ds(8 * block + shift, 8)
            for k in range(3):
                if k < 2:
                    value = ext_block(tile_of(main), top, bottom, block, k)
                else:
                    value = side_block(side_o, side_e, block)
                dst[k, at, :] = jnp.sqrt(value) if n else value

    low = jnp.where(r == 0, RIM, 0)
    high = jnp.where(r == rows - 1, RIM + TILE, EXT)
    col_ok = ((lane < 16) & (c < cols - 1)) | ((lane >= 112) & (c > 0))

    def gradient(block, carry):
        row = pl.multiple_of(8 * block, 8)
        at = pl.ds(row, 8)
        here = sub + row
        row_ok = (here >= low) & (here < high)
        cur = [ext[k, pl.ds(row + 8, 8), :] for k in range(3)]
        left = from_left(cur, 1)
        right = from_right(cur, 1)
        gx, gy = [], []
        for k in range(3):
            ok = row_ok & col_ok if k == 2 else row_ok
            gx.append(jnp.where(ok, (right[k] - left[k]) * 0.5, 0.0))
            gy.append(jnp.where(ok, (ext[k, pl.ds(row + 9, 8), :] - ext[k, pl.ds(row + 7, 8), :]) * 0.5, 0.0))
            gx_out[k, at, :] = gx[k]
            gy_out[k, at, :] = gy[k]
        for p, (a, b) in enumerate(((gx, gx), (gx, gy), (gy, gy))):
            total = window([u * v for u, v in zip(a, b)])
            for k in range(3):
                sums[p, k, at, :] = total[k]
        return carry

    lax.fori_loop(0, BLOCKS, gradient, 0, unroll=6)
    scale = mean_scale()

    def system(block, carry):
        row = pl.multiple_of(8 * block, 8)
        at = pl.ds(row, 8)
        cur = [wide[k, at, :] for k in range(3)]
        left = from_left(cur, 1)
        right = from_right(cur, 1)
        for k in range(3):
            xx, xy, yy = (tall(sums, p, k, row) * scale for p in range(3))
            if k < 2:
                for p, value in enumerate((xx, xy, yy)):
                    tensor[p, at, pl.ds(128 * k, 128)] = value
            q = cur[k]
            around = (wide[k, pl.ds(row - 1, 8), :] + wide[k, pl.ds(row + 1, 8), :]) + (left[k] + right[k])
            diag = q * around + 2.0 * COUPLING
            first, second = xx + diag, yy + diag
            over = (q * q) / (first * second - xy * xy)
            matrix[0, k, at, :] = second * over
            matrix[1, k, at, :] = xy * over
            matrix[2, k, at, :] = first * over
            inverse[k, at, :] = jnp.where(q > 0.0, 1.0 / q, 0.0)
        return carry

    lax.fori_loop(1, BLOCKS - 1, system, 0, unroll=2)


def clear_rims(ref):
    zero = jnp.zeros((8, 128), jnp.float32)
    for comp in range(2):
        for k in range(3):
            ref[comp, k, pl.ds(0, 8), :] = zero
            ref[comp, k, pl.ds(EXT - 8, 8), :] = zero


def sweep(g, rhs, matrix, block):
    row = pl.multiple_of(8 * block, 8)
    here = pl.ds(row, 8)
    sums = []
    for comp in range(2):
        cur = [g[comp, k, here, :] for k in range(3)]
        up = [g[comp, k, pl.ds(row - 1, 8), :] for k in range(3)]
        down = [g[comp, k, pl.ds(row + 1, 8), :] for k in range(3)]
        left = from_left(cur, 1)
        right = from_right(cur, 1)
        sums.append([(up[k] + down[k]) + (left[k] + right[k]) for k in range(3)])
    first, second = [], []
    for k in range(3):
        a, b, d = (matrix[i, k, here, :] for i in range(3))
        first.append(rhs[0, k, here, :] + (a * sums[0][k] - b * sums[1][k]))
        second.append(rhs[1, k, here, :] + (d * sums[1][k] - b * sums[0][k]))
    return first, second


def step(src, dst, rhs, matrix):
    def body(block, carry):
        new = sweep(src, rhs, matrix, block)
        at = pl.ds(pl.multiple_of(8 * block, 8), 8)
        for comp in range(2):
            for k in range(3):
                dst[comp, k, at, :] = new[comp][k]
        return carry

    lax.fori_loop(1, BLOCKS - 1, body, 0, unroll=17)


def first_kernel(
    ext, gx, gy, matrix, inverse, known, far, near,
    tensor, rhs, field, sent,
    chg, sums, work, fresh, sems,
):
    lane = lanes()
    zero = jnp.zeros((8, 128), jnp.float32)
    s, secs = lax.axis_index("sec"), lax.axis_size("sec")
    inner = pl.ds(RIM, TILE)
    copies = [pltpu.make_async_copy(known.at[:, inner], tensor.at[pl.ds(0, 3), 0], sems.at[0])]
    copies[0].start()

    use_far, use_near = lax.rem(s, 2) == 1, s < secs - 1

    def pick(a, b):
        return jnp.where(use_near, jnp.where(use_far, a, b), 0.0)

    def rim_rows(base):
        def read(row, cols):
            at = pl.ds(base + RIM * (cols.start // 128) + row, 8)
            return pick(far[at, :], near[at, :])

        return read

    def rim_cols(base):
        def read(row, cols):
            at = pl.ds(base + row, 8)
            return pick(far[at, :], near[at, :])

        return read

    def main(row, cols):
        at = pl.ds(RIMS + TILE * (cols.start // 128) + row, 8)
        return pick(far[at, :], near[at, :])

    top, bottom = row_halo(rim_rows(0), rim_rows(2 * RIM))
    side_o, side_e = rim_cols(4 * RIM), rim_cols(4 * RIM + STRIP)
    for block in range(BLOCKS):
        at = pl.ds(8 * block, 8)
        old = pl.ds(8 * block + 8, 8)
        for k in range(2):
            chg[k, at, :] = ext_block(main, top, bottom, block, k) - ext[k, old, :]
        chg[2, at, :] = side_block(side_o, side_e, block) - ext[2, old, :]

    def products(block, carry):
        at = pl.ds(pl.multiple_of(8 * block, 8), 8)
        for p, grad in enumerate((gx, gy)):
            total = window([grad[k, at, :] * chg[k, at, :] for k in range(3)])
            for k in range(3):
                sums[p, k, at, :] = total[k]
        return carry

    lax.fori_loop(0, BLOCKS, products, 0, unroll=6)
    scale = mean_scale()
    clear_rims(field)
    clear_rims(work)

    def right_side(block, carry):
        row = pl.multiple_of(8 * block, 8)
        at = pl.ds(row, 8)
        for k in range(3):
            xt, yt = (tall(sums, p, k, row) * scale for p in range(2))
            if k < 2:
                fresh[0, at, pl.ds(128 * k, 128)] = xt
                fresh[1, at, pl.ds(128 * k, 128)] = yt
            a, b, d = (matrix[i, k, at, :] for i in range(3))
            inv = inverse[k, at, :]
            rx = (b * yt - a * xt) * inv
            ry = (b * xt - d * yt) * inv
            rhs[0, k, at, :] = rx
            rhs[1, k, at, :] = ry
            work[0, k, at, :] = rx
            work[1, k, at, :] = ry
        return carry

    lax.fori_loop(1, BLOCKS - 1, right_side, 0, unroll=2)
    copies.append(pltpu.make_async_copy(fresh.at[:, inner], tensor.at[pl.ds(3, 2), 0], sems.at[1]))
    copies[1].start()

    step(work, field, rhs, matrix)
    step(field, work, rhs, matrix)

    def last(block, carry):
        new = sweep(work, rhs, matrix, block)
        at = pl.ds(pl.multiple_of(8 * block, 8), 8)
        for comp in range(2):
            for k in range(3):
                field[comp, k, at, :] = new[comp][k]
            for k in range(2):
                base = (2 * comp + k) * 8 * INNER
                sent[pl.ds(pl.multiple_of(base + 8 * block - 8, 8), 8), :] = new[comp][k] * inverse[k, at, :]
        return carry

    lax.fori_loop(1, BLOCKS - 1, last, 0, unroll=17)

    for comp in range(2):
        strip = [zero] * GROUP
        for block in range(INNER):
            g, place = divmod(block, GROUP)
            at = pl.ds(8 * block + 8, 8)
            tile = field[comp, 2, at, :] * inverse[2, at, :]
            tile = pltpu.roll(tile, FIELD_RIM + 16 * g, 1)
            strip[place] = jnp.where((lane >= 16 * g) & (lane < 16 * g + 16), tile, strip[place])
        for place in range(GROUP):
            sent[pl.ds(32 * INNER + STRIP * comp + 8 * place, 8), :] = strip[place]
    for copy in copies:
        copy.wait()


def second_kernel(rhs, matrix, inverse, field, far, near, out, moved, work_a, work_b, strips):
    lane = lanes()
    s = lax.axis_index("sec")
    inside = (s > 0) & (s < lax.axis_size("sec") - 1)

    def both(at):
        return jnp.where(inside, far[at, :], 0.0) + near[at, :]

    clear_rims(work_a)
    clear_rims(work_b)
    for comp in range(2):
        for block in range(INNER):
            g, place = divmod(block, GROUP)
            at = pl.ds(32 * INNER + STRIP * comp + 8 * place, 8)
            tile = pltpu.roll(both(at), 128 - FIELD_RIM - 16 * g, 1)
            strips[comp, pl.ds(8 * block, 8), :] = jnp.where((lane < FIELD_RIM) | (lane >= 128 - FIELD_RIM), tile, 0.0)

    def right_side(block, carry):
        at = pl.ds(pl.multiple_of(8 * block, 8), 8)
        for k in range(3):
            pair = []
            for comp in range(2):
                if k < 2:
                    base = (2 * comp + k) * 8 * INNER
                    rows = pl.ds(pl.multiple_of(base + 8 * block - 8, 8), 8)
                    value = both(rows)
                else:
                    value = strips[comp, pl.ds(pl.multiple_of(8 * block - 8, 8), 8), :]
                pair.append(value * (inverse[k, at, :] * COUPLING))
            a, b, d = (matrix[i, k, at, :] for i in range(3))
            moved[0, k, at, :] = rhs[0, k, at, :] + (a * pair[0] - b * pair[1])
            moved[1, k, at, :] = rhs[1, k, at, :] + (d * pair[1] - b * pair[0])
        return carry

    lax.fori_loop(1, BLOCKS - 1, right_side, 0, unroll=17)

    step(field, work_a, moved, matrix)
    step(work_a, work_b, moved, matrix)
    step(work_b, work_a, moved, matrix)

    def last(block, carry):
        new = sweep(work_a, moved, matrix, block)
        at = pl.ds(pl.multiple_of(8 * block, 8), 8)
        for comp in range(2):
            for k in range(2):
                out[comp, 0, pl.ds(pl.multiple_of(8 * block - RIM, 8), 8), pl.ds(128 * k, 128)] = (
                    new[comp][k] * inverse[k, at, :]
                )
        return carry

    lax.fori_loop(2, BLOCKS - 2, last, 0, unroll=16)


def f32(*shape):
    return jax.ShapeDtypeStruct(shape, jnp.float32)


def vmem(*shape):
    return pltpu.VMEM(shape, jnp.float32)


def call(kernel, out_shape, args, mib=6, us=0, **rest):
    return pl.pallas_call(
        kernel,
        out_shape=out_shape,
        compiler_params=pltpu.CompilerParams(vmem_limit_bytes=mib << 20),
        cost_estimate=pl.CostEstimate(flops=us * 1000000, bytes_accessed=us * 3000000, transcendentals=0),
        **rest,
    )(*args)


def local(images, stiffness):
    grid = (3, EXT, 128)
    edge, strip = f32(2 * RIM, TILE), f32(2 * STRIP, 128)
    in_hbm = pl.BlockSpec(memory_space=pltpu.HBM)
    tile = f32(1, TILE, TILE)
    images, stiffness, to_o, to_e = call(
        prepare_kernel,
        (tile, tile, edge, edge),
        [pltpu.with_memory_space_constraint(x, pltpu.HBM) for x in (images, stiffness)],
        in_specs=[in_hbm, in_hbm],
        scratch_shapes=[pltpu.SemaphoreType.DMA((2, CUTS))],
    )
    row_o = send(to_o, row_odd)
    row_e = send(to_e, row_even)

    strip_o, strip_e = call(strip_kernel, (strip, strip), (images, stiffness, row_o, row_e))
    col_o = send(strip_o, col_odd)
    col_e = send(strip_e, col_even)

    section = call(section_kernel, f32(RIMS + 2 * TILE, 128), (images, row_o, row_e, col_o, col_e))
    later_far = send(section, sec_odd)
    later_near = send(section, sec_even)
    ext, gx, gy, matrix, inverse, known = call(
        matrix_kernel,
        (f32(3, EXT + 16, 128), f32(*grid), f32(*grid), f32(3, *grid), f32(*grid), f32(3, EXT, TILE)),
        (images, stiffness, row_o, row_e, col_o, col_e),
        mib=16,
        us=4,
        scratch_shapes=[vmem(*grid), vmem(3, *grid)],
    )
    sent_rows = 32 * INNER + 2 * STRIP
    everywhere = [pl.BlockSpec(memory_space=pltpu.VMEM)] * 3
    tensor, rhs, field, sent = call(
        first_kernel,
        (f32(5, 1, TILE, TILE), f32(2, *grid), f32(2, *grid), f32(sent_rows, 128)),
        (ext, gx, gy, matrix, inverse, known, later_far, later_near),
        mib=20,
        us=5,
        out_specs=[pl.BlockSpec(memory_space=pl.ANY)] + everywhere,
        scratch_shapes=[vmem(*grid), vmem(2, *grid), vmem(2, *grid), vmem(2, EXT, TILE), pltpu.SemaphoreType.DMA((2,))],
    )

    far = send(sent, sec_odd)
    near = send(sent, sec_even)
    field = call(
        second_kernel,
        f32(2, 1, TILE, TILE),
        (rhs, matrix, inverse, field, far, near),
        mib=20,
        us=4,
        scratch_shapes=[vmem(2, *grid), vmem(2, *grid), vmem(2, *grid), vmem(2, 8 * INNER, 128)],
    )
    return tensor, field


def solution(mesh):
    in_specs = (P("sec", "row", "col"), P("sec", "row", "col"))
    out_specs = (P(None, "sec", "row", "col"), P(None, "sec", "row", "col"))
    return jax.shard_map(local, mesh=mesh, in_specs=in_specs, out_specs=out_specs, check_vma=False)
```

```python
import functools

import jax
import jax.numpy as jnp
from jax import lax
from jax.experimental import pallas as pl
from jax.experimental.pallas import tpu as pltpu
from jax.sharding import PartitionSpec as P

RADIUS = 4
COUPLING = 0.25
AXES = ("sec", "row", "col")

TILE = 256
RIM = 16
EXT = TILE + 2 * RIM
BLOCKS = EXT // 8
INNER = BLOCKS - 2
GROUP = 5
FIELD_RIM = 8
HALF = INNER // 2
FOLD = 3
SENT = 32 * HALF + 16 * FOLD
CUTS = 4
STRIP = GROUP * 8
RIMS = 4 * RIM + 2 * STRIP


def sizes():
    return [lax.axis_size(name) for name in AXES]


def even(i):
    return i ^ 1


def odd(i):
    return ((i + 1) ^ 1) - 1


def send(value, move):
    secs, rows, cols = sizes()
    found = []
    for s in range(secs):
        for r in range(rows):
            for c in range(cols):
                to = move(s, r, c, secs, rows, cols)
                found.append(((s * rows + r) * cols + c, (to[0] * rows + to[1]) * cols + to[2]))
    return lax.ppermute(value, AXES, found)


def row_even(s, r, c, secs, rows, cols):
    return s, even(r), c


def row_odd(s, r, c, secs, rows, cols):
    if 0 < r < rows - 1:
        return s, odd(r), c
    return s, r, even(c)


def col_even(s, r, c, secs, rows, cols):
    return s, r, even(c)


def col_odd(s, r, c, secs, rows, cols):
    if 0 < c < cols - 1:
        return s, r, odd(c)
    return s, even(r), c


def sec_even(s, r, c, secs, rows, cols):
    return even(s), r, c


def sec_odd(s, r, c, secs, rows, cols):
    if 0 < s < secs - 1:
        return odd(s), r, c
    return s, even(r), c


def lanes():
    return lax.broadcasted_iota(jnp.int32, (8, 128), 1)


def from_left(tiles, steps):
    rolled = [pltpu.roll(t, steps, 1) for t in tiles]
    edge = lanes() < steps
    return [jnp.where(edge, rolled[(k + 2) % 3], rolled[k]) for k in range(3)]


def from_right(tiles, steps):
    rolled = [pltpu.roll(t, 128 - steps, 1) for t in tiles]
    edge = lanes() >= 128 - steps
    return [jnp.where(edge, rolled[(k + 1) % 3], rolled[k]) for k in range(3)]


def ext_block(main, top, bottom, block, k):
    cols = pl.ds(128 * k, 128)
    if block < 2:
        return top(8 * block, cols)
    if block >= BLOCKS - 2:
        return bottom(8 * (block - (BLOCKS - 2)), cols)
    return main(8 * (block - 2), cols)


def reader(ref, offset=0):
    return lambda row, cols: ref[pl.ds(offset + row, 8), cols]


def tile_of(ref):
    return lambda row, cols: ref[0, pl.ds(row, 8), cols]


def is_odd(axis):
    return lax.rem(lax.axis_index(axis), 2) == 1


def row_halo(from_o, from_e):
    flag = is_odd("row")
    r = lax.axis_index("row")
    above, below = r > 0, r < lax.axis_size("row") - 1

    def top(row, cols):
        return jnp.where(above, jnp.where(flag, from_e(row, cols), from_o(row, cols)), 0.0)

    def bottom(row, cols):
        return jnp.where(below, jnp.where(flag, from_o(row, cols), from_e(row, cols)), 0.0)

    return top, bottom


def prepare_kernel(image, stiff, img, stf, out_o, out_e, sems):
    flag = is_odd("row")
    copies = []
    for n in range(CUTS):
        at = pl.ds(TILE // CUTS * n, TILE // CUTS)
        copies.append(pltpu.make_async_copy(image.at[0, at], img.at[0, at], sems.at[0, n]))
        copies.append(pltpu.make_async_copy(stiff.at[0, at], stf.at[0, at], sems.at[1, n]))
    for copy in copies:
        copy.start()
    for copy in copies:
        copy.wait()
    for m, ref in enumerate((img, stf)):
        for n in range(RIM // 8):
            rows = pl.ds(RIM * m + 8 * n, 8)
            a, b = ref[0, pl.ds(8 * n, 8), :], ref[0, pl.ds(TILE - RIM + 8 * n, 8), :]
            out_o[rows, :] = jnp.where(flag, b, a)
            out_e[rows, :] = jnp.where(flag, a, b)


def strip_kernel(image, stiff, row_o, row_e, out_o, out_e):
    col_flag = is_odd("col")
    lane = lanes()
    for n, main in enumerate((image, stiff)):
        top, bottom = row_halo(reader(row_o, RIM * n), reader(row_e, RIM * n))
        left = [jnp.zeros((8, 128), jnp.float32)] * GROUP
        right = [jnp.zeros((8, 128), jnp.float32)] * GROUP
        for block in range(BLOCKS):
            g, place = divmod(block, GROUP)
            here = (lane >= 16 * g) & (lane < 16 * g + 16)
            first = ext_block(tile_of(main), top, bottom, block, 0)
            last = ext_block(tile_of(main), top, bottom, block, 1)
            first = pltpu.roll(first, 16 * g, 1) if g else first
            last = pltpu.roll(last, (16 + 16 * g) % 128, 1) if g != 7 else last
            left[place] = jnp.where(here, first, left[place])
            right[place] = jnp.where(here, last, right[place])
        for place in range(GROUP):
            rows = pl.ds(STRIP * n + 8 * place, 8)
            out_o[rows, :] = jnp.where(col_flag, right[place], left[place])
            out_e[rows, :] = jnp.where(col_flag, left[place], right[place])


def rims_kernel(row_o, row_e, col_o, col_e, out):
    for m, ref in enumerate((row_o, row_e)):
        for k in range(2):
            for n in range(RIM // 8):
                out[pl.ds(RIM * (2 * m + k) + 8 * n, 8), :] = ref[pl.ds(8 * n, 8), pl.ds(128 * k, 128)]
    for m, ref in enumerate((col_o, col_e)):
        for n in range(GROUP):
            out[pl.ds(4 * RIM + STRIP * m + 8 * n, 8), :] = ref[pl.ds(8 * n, 8), :]


def side_block(from_o, from_e, block):
    lane = lanes()
    c = lax.axis_index("col")
    flag = is_odd("col")
    right_ok = (lane < 16) & (c < lax.axis_size("col") - 1)
    left_ok = (lane >= 112) & (c > 0)
    g, place = divmod(block, GROUP)
    cols = pl.ds(0, 128)
    a, b = from_o(8 * place, cols), from_e(8 * place, cols)
    right = jnp.where(flag, a, b)
    left = jnp.where(flag, b, a)
    right = pltpu.roll(right, 128 - 16 * g, 1) if g else right
    left = pltpu.roll(left, (112 - 16 * g) % 128, 1) if g != 7 else left
    return jnp.where(right_ok, right, jnp.where(left_ok, left, 0.0))


def band_kernel(start, band):
    wide = 3 * 128
    for n in range(wide // 8):
        a = lax.broadcasted_iota(jnp.int32, (8, wide), 0) + 8 * n
        b = lax.broadcasted_iota(jnp.int32, (8, wide), 1)
        apart = jnp.abs(a - b)
        near = (apart <= RADIUS) | (apart >= wide - RADIUS)
        band[pl.ds(8 * n, 8), :] = jnp.where(near, 1.0, 0.0)


def spread(prods, band, sums, count):
    ones = band[...].astype(jnp.bfloat16)
    rest = prods[...]
    total = None
    for part in range(3):
        piece = rest.astype(jnp.bfloat16)
        if part < 2:
            rest = rest - piece.astype(jnp.float32)
        found = jnp.dot(piece, ones, preferred_element_type=jnp.float32)
        total = found if total is None else total + found
    for p in range(count):
        for k in range(3):
            sums[p, k] = total[EXT * p : EXT * (p + 1), 128 * k : 128 * (k + 1)]


def tall(ref, p, k, row):
    terms = [ref[p, k, pl.ds(row + d, 8), :] for d in range(-RADIUS, RADIUS + 1)]
    while len(terms) > 1:
        terms = [sum(terms[i : i + 2]) for i in range(0, len(terms), 2)]
    return terms[0]


def mean_scale():
    keep = lax.axis_index("sec") < lax.axis_size("sec") - 1
    return jnp.where(keep, 1.0 / float((2 * RADIUS + 1) ** 2), 0.0)


def matrix_kernel(
    image, stiff, row_o, row_e, col_o, col_e, band,
    ext, gx_out, gy_out, matrix, inverse, tensor,
    wide, sums, prods,
):
    lane = lanes()
    sub = lax.broadcasted_iota(jnp.int32, (8, 128), 0)
    zero = jnp.zeros((8, 128), jnp.float32)
    r, c = lax.axis_index("row"), lax.axis_index("col")
    rows, cols = lax.axis_size("row"), lax.axis_size("col")

    for k in range(3):
        ext[k, pl.ds(0, 8), :] = zero
        ext[k, pl.ds(EXT + 8, 8), :] = zero
    for n, (main, dst, shift) in enumerate(((image, ext, 8), (stiff, wide, 0))):
        top, bottom = row_halo(reader(row_o, RIM * n), reader(row_e, RIM * n))
        side_o, side_e = reader(col_o, STRIP * n), reader(col_e, STRIP * n)
        for block in range(BLOCKS):
            at = pl.ds(8 * block + shift, 8)
            for k in range(3):
                if k < 2:
                    value = ext_block(tile_of(main), top, bottom, block, k)
                else:
                    value = side_block(side_o, side_e, block)
                dst[k, at, :] = jnp.sqrt(value) if n else value

    low = jnp.where(r == 0, RIM, 0)
    high = jnp.where(r == rows - 1, RIM + TILE, EXT)
    col_ok = ((lane < 16) & (c < cols - 1)) | ((lane >= 112) & (c > 0))

    def gradient(block, carry):
        row = pl.multiple_of(8 * block, 8)
        at = pl.ds(row, 8)
        here = sub + row
        row_ok = (here >= low) & (here < high)
        cur = [ext[k, pl.ds(row + 8, 8), :] for k in range(3)]
        left = from_left(cur, 1)
        right = from_right(cur, 1)
        gx, gy = [], []
        for k in range(3):
            ok = row_ok & col_ok if k == 2 else row_ok
            gx.append(jnp.where(ok, (right[k] - left[k]) * 0.5, 0.0))
            gy.append(jnp.where(ok, (ext[k, pl.ds(row + 9, 8), :] - ext[k, pl.ds(row + 7, 8), :]) * 0.5, 0.0))
            gx_out[k, at, :] = gx[k]
            gy_out[k, at, :] = gy[k]
        for p, (a, b) in enumerate(((gx, gx), (gx, gy), (gy, gy))):
            rows_at = pl.ds(pl.multiple_of(EXT * p + row, 8), 8)
            for k in range(3):
                prods[rows_at, pl.ds(128 * k, 128)] = a[k] * b[k]
        return carry

    lax.fori_loop(0, BLOCKS, gradient, 0, unroll=12)
    spread(prods, band, sums, 3)
    scale = mean_scale()

    def system(block, carry):
        row = pl.multiple_of(8 * block, 8)
        at = pl.ds(row, 8)
        cur = [wide[k, at, :] for k in range(3)]
        left = from_left(cur, 1)
        right = from_right(cur, 1)
        for k in range(3):
            xx, xy, yy = (tall(sums, p, k, row) * scale for p in range(3))
            if k < 2:
                for p, value in enumerate((xx, xy, yy)):
                    tensor[p, at, pl.ds(128 * k, 128)] = value
            q = cur[k]
            around = (wide[k, pl.ds(row - 1, 8), :] + wide[k, pl.ds(row + 1, 8), :]) + (left[k] + right[k])
            diag = q * around + 2.0 * COUPLING
            first, second = xx + diag, yy + diag
            over = (q * q) / (first * second - xy * xy)
            matrix[0, k, at, :] = second * over
            matrix[1, k, at, :] = xy * over
            matrix[2, k, at, :] = first * over
            inverse[k, at, :] = jnp.where(q > 0.0, 1.0 / q, 0.0)
        return carry

    lax.fori_loop(1, BLOCKS - 1, system, 0, unroll=INNER)


def clear_rims(ref):
    zero = jnp.zeros((8, 128), jnp.float32)
    for comp in range(2):
        for k in range(3):
            ref[comp, k, pl.ds(0, 8), :] = zero
            ref[comp, k, pl.ds(EXT - 8, 8), :] = zero


def sweep(g, rhs, matrix, block):
    row = pl.multiple_of(8 * block, 8)
    here = pl.ds(row, 8)
    sums = []
    for comp in range(2):
        cur = [g[comp, k, here, :] for k in range(3)]
        up = [g[comp, k, pl.ds(row - 1, 8), :] for k in range(3)]
        down = [g[comp, k, pl.ds(row + 1, 8), :] for k in range(3)]
        left = from_left(cur, 1)
        right = from_right(cur, 1)
        sums.append([(up[k] + down[k]) + (left[k] + right[k]) for k in range(3)])
    first, second = [], []
    for k in range(3):
        a, b, d = (matrix[i, k, here, :] for i in range(3))
        first.append(rhs[0, k, here, :] + (a * sums[0][k] - b * sums[1][k]))
        second.append(rhs[1, k, here, :] + (d * sums[1][k] - b * sums[0][k]))
    return first, second


def step(src, dst, rhs, matrix, low=1, high=BLOCKS - 2):
    def body(block, carry):
        new = sweep(src, rhs, matrix, block)
        at = pl.ds(pl.multiple_of(8 * block, 8), 8)
        for comp in range(2):
            for k in range(3):
                dst[comp, k, at, :] = new[comp][k]
        return carry

    lax.fori_loop(low, high + 1, body, 0, unroll=(high + 1 - low) // 2)


def first_kernel(
    ext, gx, gy, matrix, inverse, known, later_far, later_near, far, near, band,
    tensor, rhs, field, sent_a, sent_b,
    chg, sums, prods, work, fresh, sems,
):
    lane = lanes()
    zero = jnp.zeros((8, 128), jnp.float32)
    s, secs = lax.axis_index("sec"), lax.axis_size("sec")
    inner = pl.ds(RIM, TILE)
    copies = [pltpu.make_async_copy(known.at[:, inner], tensor.at[pl.ds(0, 3), 0], sems.at[0])]
    copies[0].start()

    use_far, use_near = lax.rem(s, 2) == 1, s < secs - 1

    def pick(a, b):
        return jnp.where(use_near, jnp.where(use_far, a, b), 0.0)

    def rim_rows(base):
        def read(row, cols):
            at = pl.ds(base + RIM * (cols.start // 128) + row, 8)
            return pick(far[at, :], near[at, :])

        return read

    def rim_cols(base):
        def read(row, cols):
            at = pl.ds(base + row, 8)
            return pick(far[at, :], near[at, :])

        return read

    def main(row, cols):
        at = pl.ds(row, 8)
        return pick(later_far[0, at, cols], later_near[0, at, cols])

    top, bottom = row_halo(rim_rows(0), rim_rows(2 * RIM))
    side_o, side_e = rim_cols(4 * RIM), rim_cols(4 * RIM + STRIP)
    for block in range(BLOCKS):
        at = pl.ds(8 * block, 8)
        old = pl.ds(8 * block + 8, 8)
        for k in range(2):
            chg[k, at, :] = ext_block(main, top, bottom, block, k) - ext[k, old, :]
        chg[2, at, :] = side_block(side_o, side_e, block) - ext[2, old, :]

    def products(block, carry):
        row = pl.multiple_of(8 * block, 8)
        at = pl.ds(row, 8)
        for p, grad in enumerate((gx, gy)):
            rows_at = pl.ds(pl.multiple_of(EXT * p + row, 8), 8)
            for k in range(3):
                prods[rows_at, pl.ds(128 * k, 128)] = grad[k, at, :] * chg[k, at, :]
        return carry

    lax.fori_loop(0, BLOCKS, products, 0, unroll=6)
    spread(prods, band, sums, 2)
    scale = mean_scale()
    clear_rims(field)
    clear_rims(work)

    def right_side(block, carry):
        row = pl.multiple_of(8 * block, 8)
        at = pl.ds(row, 8)
        for k in range(3):
            xt, yt = (tall(sums, p, k, row) * scale for p in range(2))
            if k < 2:
                fresh[0, at, pl.ds(128 * k, 128)] = xt
                fresh[1, at, pl.ds(128 * k, 128)] = yt
            a, b, d = (matrix[i, k, at, :] for i in range(3))
            inv = inverse[k, at, :]
            rx = (b * yt - a * xt) * inv
            ry = (b * xt - d * yt) * inv
            rhs[0, k, at, :] = rx
            rhs[1, k, at, :] = ry
            work[0, k, at, :] = rx
            work[1, k, at, :] = ry
        return carry

    lax.fori_loop(1, BLOCKS - 1, right_side, 0, unroll=17)
    copies.append(pltpu.make_async_copy(fresh.at[:, inner], tensor.at[pl.ds(3, 2), 0], sems.at[1]))
    copies[1].start()

    step(work, field, rhs, matrix)
    step(field, work, rhs, matrix)

    for half, sent in enumerate((sent_a, sent_b)):
        start = 1 + HALF * half

        def last(block, carry):
            new = sweep(work, rhs, matrix, block)
            at = pl.ds(pl.multiple_of(8 * block, 8), 8)
            for comp in range(2):
                for k in range(3):
                    field[comp, k, at, :] = new[comp][k]
                for k in range(2):
                    to = pl.multiple_of(8 * ((2 * comp + k) * HALF + block - start), 8)
                    sent[pl.ds(to, 8), :] = new[comp][k] * inverse[k, at, :]
            return carry

        lax.fori_loop(start, start + HALF, last, 0, unroll=HALF)

        for comp in range(2):
            strip = [zero] * FOLD
            for n in range(HALF):
                g, place = divmod(n, FOLD)
                at = pl.ds(8 * (start + n), 8)
                tile = pltpu.roll(field[comp, 2, at, :] * inverse[2, at, :], FIELD_RIM + 16 * g, 1)
                strip[place] = jnp.where((lane >= 16 * g) & (lane < 16 * g + 16), tile, strip[place])
            for place in range(FOLD):
                sent[pl.ds(32 * HALF + 8 * (FOLD * comp + place), 8), :] = strip[place]
    for copy in copies:
        copy.wait()


def beside_terms(half, received, matrix, inverse, strips, store, ok=None):
    lane = lanes()
    start = 1 + HALF * half

    def read(at):
        return received[at, :] if ok is None else jnp.where(ok, received[at, :], 0.0)

    for comp in range(2):
        for n in range(HALF):
            g, place = divmod(n, FOLD)
            tile = read(pl.ds(32 * HALF + 8 * (FOLD * comp + place), 8))
            tile = pltpu.roll(tile, 128 - FIELD_RIM - 16 * g, 1)
            strips[comp, pl.ds(8 * n, 8), :] = jnp.where((lane < FIELD_RIM) | (lane >= 128 - FIELD_RIM), tile, 0.0)

    def body(n, carry):
        at = pl.ds(pl.multiple_of(8 * (start + n), 8), 8)
        for k in range(3):
            pair = []
            for comp in range(2):
                if k < 2:
                    value = read(pl.ds(pl.multiple_of(8 * ((2 * comp + k) * HALF + n), 8), 8))
                else:
                    value = strips[comp, pl.ds(pl.multiple_of(8 * n, 8), 8), :]
                pair.append(value * (inverse[k, at, :] * COUPLING))
            a, b, d = (matrix[i, k, at, :] for i in range(3))
            store(k, at, a * pair[0] - b * pair[1], d * pair[1] - b * pair[0])
        return carry

    lax.fori_loop(0, HALF, body, 0, unroll=HALF)


def carry_kernel(rhs, matrix, inverse, field, near_a, near_b, out, moved, work_a, work_b, strips):
    clear_rims(work_a)
    clear_rims(work_b)

    def store(k, at, x, y):
        moved[0, k, at, :] = rhs[0, k, at, :] + x
        moved[1, k, at, :] = rhs[1, k, at, :] + y

    for half, near in enumerate((near_a, near_b)):
        beside_terms(half, near, matrix, inverse, strips, store)
    step(field, work_a, moved, matrix)
    step(work_a, work_b, moved, matrix)
    step(work_b, work_a, moved, matrix)

    def last(block, carry):
        new = sweep(work_a, moved, matrix, block)
        at = pl.ds(pl.multiple_of(8 * block, 8), 8)
        for comp in range(2):
            for k in range(2):
                out[comp, k, at, :] = new[comp][k]
        return carry

    lax.fori_loop(2, BLOCKS - 2, last, 0, unroll=16)


def second_kernel(half, matrix, inverse, carried, far, *rest):
    if half == 0:
        out, seam, moved, work_a, work_b, strips, result, sems = rest
    else:
        seam, _, out, moved, work_a, work_b, strips, result, sems = rest
    s = lax.axis_index("sec")
    inside = (s > 0) & (s < lax.axis_size("sec") - 1)
    low, high = (1, HALF + 1) if half == 0 else (HALF, 2 * HALF)
    zero = jnp.zeros((8, 128), jnp.float32)
    for comp in range(2):
        for k in range(3):
            for ref in (moved, work_a, work_b):
                ref[comp, k, pl.ds(8 * low - 8, 8), :] = zero
                ref[comp, k, pl.ds(8 * high + 8, 8), :] = zero
            moved[comp, k, pl.ds(8 * (high if half == 0 else low), 8), :] = zero

    def store(k, at, x, y):
        moved[0, k, at, :] = x
        moved[1, k, at, :] = y

    beside_terms(half, far, matrix, inverse, strips, store, inside)
    step(moved, work_a, moved, matrix, low, high)
    step(work_a, work_b, moved, matrix, low, high)

    first, count = (2, HALF - 2) if half == 0 else (HALF, HALF)
    moves = []

    def final(block, new):
        at = pl.ds(8 * block, 8)
        for comp in range(2):
            for k in range(2):
                value = new[comp][k] + carried[comp, k, at, :]
                if half == 1 and block <= HALF + 1:
                    value = value + seam[comp, k, pl.ds(8 * (block - HALF), 8), :]
                result[comp, pl.ds(8 * block - RIM, 8), pl.ds(128 * k, 128)] = value * inverse[k, at, :]

    for block in range(max(low, 2), min(high, BLOCKS - 3) + 1):
        new = sweep(work_b, moved, matrix, block)
        if block < first + count:
            final(block, new)
        else:
            for comp in range(2):
                for k in range(2):
                    seam[comp, k, pl.ds(8 * (block - HALF), 8), :] = new[comp][k]
        if block + 1 == first + count or (block + 1 - first) % 8 == 0 and block < first + count:
            done = len(moves) // 2
            at = pl.ds(8 * (first + 8 * done) - RIM, 8 * (block + 1 - first - 8 * done))
            for c in range(2):
                moves.append(pltpu.make_async_copy(result.at[c, at], out.at[c, 0, at], sems.at[c, done]))
                moves[-1].start()
    for move in moves:
        move.wait()


def f32(*shape):
    return jax.ShapeDtypeStruct(shape, jnp.float32)


def vmem(*shape):
    return pltpu.VMEM(shape, jnp.float32)


def call(kernel, out_shape, args, mib=6, us=0, **rest):
    return pl.pallas_call(
        kernel,
        out_shape=out_shape,
        compiler_params=pltpu.CompilerParams(vmem_limit_bytes=mib << 20),
        cost_estimate=pl.CostEstimate(flops=us * 1000000, bytes_accessed=us * 3000000, transcendentals=0),
        **rest,
    )(*args)


def local(images, stiffness):
    grid = (3, EXT, 128)
    edge, strip = f32(2 * RIM, TILE), f32(2 * STRIP, 128)
    later_far = send(images, sec_odd)
    later_near = send(images, sec_even)
    in_hbm = pl.BlockSpec(memory_space=pltpu.HBM)
    tile = f32(1, TILE, TILE)
    images, stiffness, to_o, to_e = call(
        prepare_kernel,
        (tile, tile, edge, edge),
        [pltpu.with_memory_space_constraint(x, pltpu.HBM) for x in (images, stiffness)],
        in_specs=[in_hbm, in_hbm],
        scratch_shapes=[pltpu.SemaphoreType.DMA((2, CUTS))],
    )
    row_o = send(to_o, row_odd)
    row_e = send(to_e, row_even)

    strip_o, strip_e = call(strip_kernel, (strip, strip), (images, stiffness, row_o, row_e))
    col_o = send(strip_o, col_odd)
    col_e = send(strip_e, col_even)

    band = call(band_kernel, f32(3 * 128, 3 * 128), (to_o,), us=1)

    rims = call(rims_kernel, f32(RIMS, 128), (row_o, row_e, col_o, col_e))
    rims_far = send(rims, sec_odd)
    rims_near = send(rims, sec_even)
    ext, gx, gy, matrix, inverse, known = call(
        matrix_kernel,
        (f32(3, EXT + 16, 128), f32(*grid), f32(*grid), f32(3, *grid), f32(*grid), f32(3, EXT, TILE)),
        (images, stiffness, row_o, row_e, col_o, col_e, band),
        mib=20,
        us=4,
        scratch_shapes=[vmem(*grid), vmem(3, *grid), vmem(3 * EXT, 3 * 128)],
    )
    everywhere = [pl.BlockSpec(memory_space=pltpu.VMEM)] * 4
    tensor, rhs, field, sent_a, sent_b = call(
        first_kernel,
        (f32(5, 1, TILE, TILE), f32(2, *grid), f32(2, *grid), f32(SENT, 128), f32(SENT, 128)),
        (ext, gx, gy, matrix, inverse, known, later_far, later_near, rims_far, rims_near, band),
        mib=20,
        us=5,
        out_specs=[pl.BlockSpec(memory_space=pl.ANY)] + everywhere,
        scratch_shapes=[
            vmem(*grid),
            vmem(2, *grid),
            vmem(2 * EXT, 3 * 128),
            vmem(2, *grid),
            vmem(2, EXT, TILE),
            pltpu.SemaphoreType.DMA((2,)),
        ],
    )

    near_a, near_b = send(sent_a, sec_even), send(sent_b, sec_even)
    far_a, far_b = send(sent_a, sec_odd), send(sent_b, sec_odd)
    carried = call(
        carry_kernel,
        f32(2, 2, EXT, 128),
        (rhs, matrix, inverse, field, near_a, near_b),
        mib=16,
        us=3,
        scratch_shapes=[vmem(2, *grid), vmem(2, *grid), vmem(2, *grid), vmem(2, 8 * HALF, 128)],
    )
    whole = pl.BlockSpec(memory_space=pltpu.VMEM)
    anywhere = pl.BlockSpec(memory_space=pl.ANY)
    final = f32(2, 1, TILE, TILE)
    scratch = [
        vmem(2, *grid),
        vmem(2, *grid),
        vmem(2, *grid),
        vmem(2, 8 * HALF, 128),
        vmem(2, TILE, TILE),
        pltpu.SemaphoreType.DMA((2, CUTS)),
    ]
    field, seam = call(
        functools.partial(second_kernel, 0),
        (final, f32(2, 2, 16, 128)),
        (matrix, inverse, carried, far_a),
        mib=16,
        us=2,
        out_specs=[anywhere, whole],
        scratch_shapes=scratch,
    )
    field = call(
        functools.partial(second_kernel, 1),
        final,
        (matrix, inverse, carried, far_b, seam, field),
        mib=16,
        us=2,
        in_specs=[whole] * 5 + [anywhere],
        out_specs=anywhere,
        input_output_aliases={5: 0},
        scratch_shapes=scratch,
    )
    return tensor, field


def solution(mesh):
    in_specs = (P("sec", "row", "col"), P("sec", "row", "col"))
    out_specs = (P(None, "sec", "row", "col"), P(None, "sec", "row", "col"))
    return jax.shard_map(local, mesh=mesh, in_specs=in_specs, out_specs=out_specs, check_vma=False)
```

```python
import functools

import jax
import jax.numpy as jnp
from jax import lax
from jax.experimental import pallas as pl
from jax.experimental.pallas import tpu as pltpu
from jax.sharding import PartitionSpec as P

RADIUS = 4
COUPLING = 0.25
AXES = ("sec", "row", "col")

TILE = 256
RIM = 16
EXT = TILE + 2 * RIM
BLOCKS = EXT // 8
INNER = BLOCKS - 2
GROUP = 5
FIELD_RIM = 8
COUNTS = (22, INNER - 22)
STARTS = (1, 1 + COUNTS[0])
FOLD = 3
SENT = [32 * count + 16 * FOLD for count in COUNTS]
CUTS = 4
STRIP = GROUP * 8
RIMS = 4 * RIM + 2 * STRIP


def sizes():
    return [lax.axis_size(name) for name in AXES]


def even(i):
    return i ^ 1


def odd(i):
    return ((i + 1) ^ 1) - 1


def send(value, move):
    secs, rows, cols = sizes()
    found = []
    for s in range(secs):
        for r in range(rows):
            for c in range(cols):
                to = move(s, r, c, secs, rows, cols)
                found.append(((s * rows + r) * cols + c, (to[0] * rows + to[1]) * cols + to[2]))
    return lax.ppermute(value, AXES, found)


def row_even(s, r, c, secs, rows, cols):
    return s, even(r), c


def row_odd(s, r, c, secs, rows, cols):
    if 0 < r < rows - 1:
        return s, odd(r), c
    return s, r, even(c)


def col_even(s, r, c, secs, rows, cols):
    return s, r, even(c)


def col_odd(s, r, c, secs, rows, cols):
    if 0 < c < cols - 1:
        return s, r, odd(c)
    return s, even(r), c


def sec_even(s, r, c, secs, rows, cols):
    return even(s), r, c


def sec_odd(s, r, c, secs, rows, cols):
    if 0 < s < secs - 1:
        return odd(s), r, c
    return s, even(r), c


def lanes():
    return lax.broadcasted_iota(jnp.int32, (8, 128), 1)


def from_left(tiles, steps):
    rolled = [pltpu.roll(t, steps, 1) for t in tiles]
    edge = lanes() < steps
    return [jnp.where(edge, rolled[(k + 2) % 3], rolled[k]) for k in range(3)]


def from_right(tiles, steps):
    rolled = [pltpu.roll(t, 128 - steps, 1) for t in tiles]
    edge = lanes() >= 128 - steps
    return [jnp.where(edge, rolled[(k + 1) % 3], rolled[k]) for k in range(3)]


def ext_block(main, top, bottom, block, k):
    cols = pl.ds(128 * k, 128)
    if block < 2:
        return top(8 * block, cols)
    if block >= BLOCKS - 2:
        return bottom(8 * (block - (BLOCKS - 2)), cols)
    return main(8 * (block - 2), cols)


def reader(ref, offset=0):
    return lambda row, cols: ref[pl.ds(offset + row, 8), cols]


def tile_of(ref):
    return lambda row, cols: ref[0, pl.ds(row, 8), cols]


def is_odd(axis):
    return lax.rem(lax.axis_index(axis), 2) == 1


def row_halo(from_o, from_e):
    flag = is_odd("row")
    r = lax.axis_index("row")
    above, below = r > 0, r < lax.axis_size("row") - 1

    def top(row, cols):
        return jnp.where(above, jnp.where(flag, from_e(row, cols), from_o(row, cols)), 0.0)

    def bottom(row, cols):
        return jnp.where(below, jnp.where(flag, from_o(row, cols), from_e(row, cols)), 0.0)

    return top, bottom


def edges_kernel(image, stiff, out_o, out_e, first, last, sems):
    flag = is_odd("row")
    copies = []
    for m, ref in enumerate((image, stiff)):
        for n, (dst, at) in enumerate(((first, 0), (last, TILE - RIM))):
            copies.append(pltpu.make_async_copy(ref.at[0, pl.ds(at, RIM)], dst.at[pl.ds(RIM * m, RIM)], sems.at[m, n]))
    for copy in copies:
        copy.start()
    for copy in copies:
        copy.wait()
    for n in range(2 * RIM // 8):
        rows = pl.ds(8 * n, 8)
        a, b = first[rows, :], last[rows, :]
        out_o[rows, :] = jnp.where(flag, b, a)
        out_e[rows, :] = jnp.where(flag, a, b)


def load_kernel(image, stiff, after, img, stf, sems):
    copies = []
    for n in range(CUTS):
        at = pl.ds(TILE // CUTS * n, TILE // CUTS)
        copies.append(pltpu.make_async_copy(image.at[0, at], img.at[0, at], sems.at[0, n]))
        copies.append(pltpu.make_async_copy(stiff.at[0, at], stf.at[0, at], sems.at[1, n]))
    for copy in copies:
        copy.start()
    for copy in copies:
        copy.wait()


def strip_kernel(image, stiff, row_o, row_e, out_o, out_e):
    col_flag = is_odd("col")
    lane = lanes()
    for n, main in enumerate((image, stiff)):
        top, bottom = row_halo(reader(row_o, RIM * n), reader(row_e, RIM * n))
        left = [jnp.zeros((8, 128), jnp.float32)] * GROUP
        right = [jnp.zeros((8, 128), jnp.float32)] * GROUP
        for block in range(BLOCKS):
            g, place = divmod(block, GROUP)
            here = (lane >= 16 * g) & (lane < 16 * g + 16)
            first = ext_block(tile_of(main), top, bottom, block, 0)
            last = ext_block(tile_of(main), top, bottom, block, 1)
            first = pltpu.roll(first, 16 * g, 1) if g else first
            last = pltpu.roll(last, (16 + 16 * g) % 128, 1) if g != 7 else last
            left[place] = jnp.where(here, first, left[place])
            right[place] = jnp.where(here, last, right[place])
        for place in range(GROUP):
            rows = pl.ds(STRIP * n + 8 * place, 8)
            out_o[rows, :] = jnp.where(col_flag, right[place], left[place])
            out_e[rows, :] = jnp.where(col_flag, left[place], right[place])


def rims_kernel(row_o, row_e, col_o, col_e, out):
    for m, ref in enumerate((row_o, row_e)):
        for k in range(2):
            for n in range(RIM // 8):
                out[pl.ds(RIM * (2 * m + k) + 8 * n, 8), :] = ref[pl.ds(8 * n, 8), pl.ds(128 * k, 128)]
    for m, ref in enumerate((col_o, col_e)):
        for n in range(GROUP):
            out[pl.ds(4 * RIM + STRIP * m + 8 * n, 8), :] = ref[pl.ds(8 * n, 8), :]


def side_block(from_o, from_e, block):
    lane = lanes()
    c = lax.axis_index("col")
    flag = is_odd("col")
    right_ok = (lane < 16) & (c < lax.axis_size("col") - 1)
    left_ok = (lane >= 112) & (c > 0)
    g, place = divmod(block, GROUP)
    cols = pl.ds(0, 128)
    a, b = from_o(8 * place, cols), from_e(8 * place, cols)
    right = jnp.where(flag, a, b)
    left = jnp.where(flag, b, a)
    right = pltpu.roll(right, 128 - 16 * g, 1) if g else right
    left = pltpu.roll(left, (112 - 16 * g) % 128, 1) if g != 7 else left
    return jnp.where(right_ok, right, jnp.where(left_ok, left, 0.0))


def band_kernel(start, band):
    wide = 3 * 128
    for n in range(wide // 8):
        a = lax.broadcasted_iota(jnp.int32, (8, wide), 0) + 8 * n
        b = lax.broadcasted_iota(jnp.int32, (8, wide), 1)
        apart = jnp.abs(a - b)
        near = (apart <= RADIUS) | (apart >= wide - RADIUS)
        band[pl.ds(8 * n, 8), :] = jnp.where(near, 1.0, 0.0)


def spread(prods, band, sums, count):
    ones = band[...].astype(jnp.bfloat16)
    rest = prods[...]
    total = None
    for part in range(3):
        piece = rest.astype(jnp.bfloat16)
        if part < 2:
            rest = rest - piece.astype(jnp.float32)
        found = jnp.dot(piece, ones, preferred_element_type=jnp.float32)
        total = found if total is None else total + found
    for p in range(count):
        for k in range(3):
            sums[p, k] = total[EXT * p : EXT * (p + 1), 128 * k : 128 * (k + 1)]


def tall(ref, p, k, row):
    terms = [ref[p, k, pl.ds(row + d, 8), :] for d in range(-RADIUS, RADIUS + 1)]
    while len(terms) > 1:
        terms = [sum(terms[i : i + 2]) for i in range(0, len(terms), 2)]
    return terms[0]


def mean_scale():
    keep = lax.axis_index("sec") < lax.axis_size("sec") - 1
    return jnp.where(keep, 1.0 / float((2 * RADIUS + 1) ** 2), 0.0)


def matrix_kernel(
    image, stiff, row_o, row_e, col_o, col_e, band,
    ext, gx_out, gy_out, matrix, inverse, tensor,
    wide, sums, prods,
):
    lane = lanes()
    sub = lax.broadcasted_iota(jnp.int32, (8, 128), 0)
    zero = jnp.zeros((8, 128), jnp.float32)
    r, c = lax.axis_index("row"), lax.axis_index("col")
    rows, cols = lax.axis_size("row"), lax.axis_size("col")

    for k in range(3):
        ext[k, pl.ds(0, 8), :] = zero
        ext[k, pl.ds(EXT + 8, 8), :] = zero
    for n, (main, dst, shift) in enumerate(((image, ext, 8), (stiff, wide, 0))):
        top, bottom = row_halo(reader(row_o, RIM * n), reader(row_e, RIM * n))
        side_o, side_e = reader(col_o, STRIP * n), reader(col_e, STRIP * n)
        for block in range(BLOCKS):
            at = pl.ds(8 * block + shift, 8)
            for k in range(3):
                if k < 2:
                    value = ext_block(tile_of(main), top, bottom, block, k)
                else:
                    value = side_block(side_o, side_e, block)
                dst[k, at, :] = jnp.sqrt(value) if n else value

    low = jnp.where(r == 0, RIM, 0)
    high = jnp.where(r == rows - 1, RIM + TILE, EXT)
    col_ok = ((lane < 16) & (c < cols - 1)) | ((lane >= 112) & (c > 0))

    def gradient(block, carry):
        row = pl.multiple_of(8 * block, 8)
        at = pl.ds(row, 8)
        here = sub + row
        row_ok = (here >= low) & (here < high)
        cur = [ext[k, pl.ds(row + 8, 8), :] for k in range(3)]
        left = from_left(cur, 1)
        right = from_right(cur, 1)
        gx, gy = [], []
        for k in range(3):
            ok = row_ok & col_ok if k == 2 else row_ok
            gx.append(jnp.where(ok, (right[k] - left[k]) * 0.5, 0.0))
            gy.append(jnp.where(ok, (ext[k, pl.ds(row + 9, 8), :] - ext[k, pl.ds(row + 7, 8), :]) * 0.5, 0.0))
            gx_out[k, at, :] = gx[k]
            gy_out[k, at, :] = gy[k]
        for p, (a, b) in enumerate(((gx, gx), (gx, gy), (gy, gy))):
            rows_at = pl.ds(pl.multiple_of(EXT * p + row, 8), 8)
            for k in range(3):
                prods[rows_at, pl.ds(128 * k, 128)] = a[k] * b[k]
        return carry

    lax.fori_loop(0, BLOCKS, gradient, 0, unroll=12)
    spread(prods, band, sums, 3)
    scale = mean_scale()

    def system(block, carry):
        row = pl.multiple_of(8 * block, 8)
        at = pl.ds(row, 8)
        cur = [wide[k, at, :] for k in range(3)]
        left = from_left(cur, 1)
        right = from_right(cur, 1)
        for k in range(3):
            xx, xy, yy = (tall(sums, p, k, row) * scale for p in range(3))
            if k < 2:
                for p, value in enumerate((xx, xy, yy)):
                    tensor[p, at, pl.ds(128 * k, 128)] = value
            q = cur[k]
            around = (wide[k, pl.ds(row - 1, 8), :] + wide[k, pl.ds(row + 1, 8), :]) + (left[k] + right[k])
            diag = q * around + 2.0 * COUPLING
            first, second = xx + diag, yy + diag
            over = (q * q) / (first * second - xy * xy)
            matrix[0, k, at, :] = second * over
            matrix[1, k, at, :] = xy * over
            matrix[2, k, at, :] = first * over
            inverse[k, at, :] = jnp.where(q > 0.0, 1.0 / q, 0.0)
        return carry

    lax.fori_loop(1, BLOCKS - 1, system, 0, unroll=INNER)


def clear_rims(ref):
    zero = jnp.zeros((8, 128), jnp.float32)
    for comp in range(2):
        for k in range(3):
            ref[comp, k, pl.ds(0, 8), :] = zero
            ref[comp, k, pl.ds(EXT - 8, 8), :] = zero


def sweep(g, rhs, matrix, block):
    row = pl.multiple_of(8 * block, 8)
    here = pl.ds(row, 8)
    sums = []
    for comp in range(2):
        cur = [g[comp, k, here, :] for k in range(3)]
        up = [g[comp, k, pl.ds(row - 1, 8), :] for k in range(3)]
        down = [g[comp, k, pl.ds(row + 1, 8), :] for k in range(3)]
        left = from_left(cur, 1)
        right = from_right(cur, 1)
        sums.append([(up[k] + down[k]) + (left[k] + right[k]) for k in range(3)])
    first, second = [], []
    for k in range(3):
        a, b, d = (matrix[i, k, here, :] for i in range(3))
        first.append(rhs[0, k, here, :] + (a * sums[0][k] - b * sums[1][k]))
        second.append(rhs[1, k, here, :] + (d * sums[1][k] - b * sums[0][k]))
    return first, second


def step(src, dst, rhs, matrix, low=1, high=BLOCKS - 2, unroll=INNER // 2):
    def body(block, carry):
        new = sweep(src, rhs, matrix, block)
        at = pl.ds(pl.multiple_of(8 * block, 8), 8)
        for comp in range(2):
            for k in range(3):
                dst[comp, k, at, :] = new[comp][k]
        return carry

    lax.fori_loop(low, high + 1, body, 0, unroll=unroll)


def first_kernel(
    ext, gx, gy, matrix, inverse, known, later_far, later_near, far, near, band,
    tensor, rhs, field, sent_a, sent_b, sent,
    chg, sums, prods, work, fresh, sems,
):
    lane = lanes()
    zero = jnp.zeros((8, 128), jnp.float32)
    s, secs = lax.axis_index("sec"), lax.axis_size("sec")
    inner = pl.ds(RIM, TILE)
    copies = [pltpu.make_async_copy(known.at[:, inner], tensor.at[pl.ds(0, 3), 0], sems.at[0])]
    copies[0].start()

    use_far, use_near = lax.rem(s, 2) == 1, s < secs - 1

    def pick(a, b):
        return jnp.where(use_near, jnp.where(use_far, a, b), 0.0)

    def rim_rows(base):
        def read(row, cols):
            at = pl.ds(base + RIM * (cols.start // 128) + row, 8)
            return pick(far[at, :], near[at, :])

        return read

    def rim_cols(base):
        def read(row, cols):
            at = pl.ds(base + row, 8)
            return pick(far[at, :], near[at, :])

        return read

    def main(row, cols):
        at = pl.ds(row, 8)
        return pick(later_far[0, at, cols], later_near[0, at, cols])

    top, bottom = row_halo(rim_rows(0), rim_rows(2 * RIM))
    side_o, side_e = rim_cols(4 * RIM), rim_cols(4 * RIM + STRIP)
    for block in range(BLOCKS):
        at = pl.ds(8 * block, 8)
        old = pl.ds(8 * block + 8, 8)
        for k in range(2):
            chg[k, at, :] = ext_block(main, top, bottom, block, k) - ext[k, old, :]
        chg[2, at, :] = side_block(side_o, side_e, block) - ext[2, old, :]

    def products(block, carry):
        row = pl.multiple_of(8 * block, 8)
        at = pl.ds(row, 8)
        for p, grad in enumerate((gx, gy)):
            rows_at = pl.ds(pl.multiple_of(EXT * p + row, 8), 8)
            for k in range(3):
                prods[rows_at, pl.ds(128 * k, 128)] = grad[k, at, :] * chg[k, at, :]
        return carry

    lax.fori_loop(0, BLOCKS, products, 0, unroll=6)
    spread(prods, band, sums, 2)
    scale = mean_scale()
    clear_rims(field)
    clear_rims(work)

    def right_side(block, carry):
        row = pl.multiple_of(8 * block, 8)
        at = pl.ds(row, 8)
        for k in range(3):
            xt, yt = (tall(sums, p, k, row) * scale for p in range(2))
            if k < 2:
                fresh[0, at, pl.ds(128 * k, 128)] = xt
                fresh[1, at, pl.ds(128 * k, 128)] = yt
            a, b, d = (matrix[i, k, at, :] for i in range(3))
            inv = inverse[k, at, :]
            rx = (b * yt - a * xt) * inv
            ry = (b * xt - d * yt) * inv
            rhs[0, k, at, :] = rx
            rhs[1, k, at, :] = ry
            work[0, k, at, :] = rx
            work[1, k, at, :] = ry
        return carry

    lax.fori_loop(1, BLOCKS - 1, right_side, 0, unroll=17)
    copies.append(pltpu.make_async_copy(fresh.at[:, inner], tensor.at[pl.ds(3, 2), 0], sems.at[1]))
    copies[1].start()

    step(work, field, rhs, matrix)
    step(field, work, rhs, matrix)

    for half, part in enumerate((sent_a, sent_b)):
        start, count, base = STARTS[half], COUNTS[half], SENT[0] * half

        def last(block, carry):
            new = sweep(work, rhs, matrix, block)
            at = pl.ds(pl.multiple_of(8 * block, 8), 8)
            for comp in range(2):
                for k in range(3):
                    field[comp, k, at, :] = new[comp][k]
                for k in range(2):
                    to = pl.multiple_of(8 * ((2 * comp + k) * count + block - start), 8)
                    value = new[comp][k] * inverse[k, at, :]
                    part[pl.ds(to, 8), :] = value
                    sent[pl.ds(pl.multiple_of(base + to, 8), 8), :] = value
            return carry

        lax.fori_loop(start, start + count, last, 0, unroll=count)

        for comp in range(2):
            strip = [zero] * FOLD
            for n in range(count):
                g, place = divmod(n, FOLD)
                at = pl.ds(8 * (start + n), 8)
                tile = pltpu.roll(field[comp, 2, at, :] * inverse[2, at, :], FIELD_RIM + 16 * g, 1)
                strip[place] = jnp.where((lane >= 16 * g) & (lane < 16 * g + 16), tile, strip[place])
            for place in range(FOLD):
                for ref, at in ((part, 0), (sent, base)):
                    ref[pl.ds(at + 32 * count + 8 * (FOLD * comp + place), 8), :] = strip[place]
    for copy in copies:
        copy.wait()


def beside_terms(half, received, matrix, inverse, strips, store, base=0, ok=None):
    lane = lanes()
    start, count = STARTS[half], COUNTS[half]

    def read(at):
        return received[at, :] if ok is None else jnp.where(ok, received[at, :], 0.0)

    for comp in range(2):
        for n in range(count):
            g, place = divmod(n, FOLD)
            tile = read(pl.ds(base + 32 * count + 8 * (FOLD * comp + place), 8))
            tile = pltpu.roll(tile, 128 - FIELD_RIM - 16 * g, 1)
            strips[comp, pl.ds(8 * n, 8), :] = jnp.where((lane < FIELD_RIM) | (lane >= 128 - FIELD_RIM), tile, 0.0)

    def body(n, carry):
        at = pl.ds(pl.multiple_of(8 * (start + n), 8), 8)
        for k in range(3):
            pair = []
            for comp in range(2):
                if k < 2:
                    value = read(pl.ds(pl.multiple_of(base + 8 * ((2 * comp + k) * count + n), 8), 8))
                else:
                    value = strips[comp, pl.ds(pl.multiple_of(8 * n, 8), 8), :]
                pair.append(value * (inverse[k, at, :] * COUPLING))
            a, b, d = (matrix[i, k, at, :] for i in range(3))
            store(k, at, a * pair[0] - b * pair[1], d * pair[1] - b * pair[0])
        return carry

    lax.fori_loop(0, count, body, 0, unroll=count)


def carry_kernel(rhs, matrix, inverse, field, near, out, moved, work_a, work_b, strips):
    clear_rims(work_a)
    clear_rims(work_b)

    def store(k, at, x, y):
        moved[0, k, at, :] = rhs[0, k, at, :] + x
        moved[1, k, at, :] = rhs[1, k, at, :] + y

    for half in range(2):
        beside_terms(half, near, matrix, inverse, strips, store, SENT[0] * half)
    step(field, work_a, moved, matrix)
    step(work_a, work_b, moved, matrix)
    step(work_b, work_a, moved, matrix)

    def last(block, carry):
        new = sweep(work_a, moved, matrix, block)
        at = pl.ds(pl.multiple_of(8 * block, 8), 8)
        for comp in range(2):
            for k in range(2):
                out[comp, k, at, :] = new[comp][k]
        return carry

    lax.fori_loop(2, BLOCKS - 2, last, 0, unroll=16)


def second_kernel(half, matrix, inverse, carried, far, *rest):
    if half == 0:
        out, seam, moved, work_a, work_b, strips, result, sems = rest
    else:
        seam, _, out, moved, work_a, work_b, strips, result, sems = rest
    s = lax.axis_index("sec")
    inside = (s > 0) & (s < lax.axis_size("sec") - 1)
    edge = COUNTS[0]
    low, high = (1, edge + 1) if half == 0 else (edge, INNER)
    zero = jnp.zeros((8, 128), jnp.float32)
    for comp in range(2):
        for k in range(3):
            for ref in (moved, work_a, work_b):
                ref[comp, k, pl.ds(8 * low - 8, 8), :] = zero
                ref[comp, k, pl.ds(8 * high + 8, 8), :] = zero
            moved[comp, k, pl.ds(8 * (high if half == 0 else low), 8), :] = zero

    def store(k, at, x, y):
        moved[0, k, at, :] = x
        moved[1, k, at, :] = y

    beside_terms(half, far, matrix, inverse, strips, store, ok=inside)
    step(moved, work_a, moved, matrix, low, high, high + 1 - low)
    step(work_a, work_b, moved, matrix, low, high, high + 1 - low)

    first, count = (2, edge - 2) if half == 0 else (edge, INNER - edge)
    moves = []

    def final(block, new):
        at = pl.ds(8 * block, 8)
        for comp in range(2):
            for k in range(2):
                value = new[comp][k] + carried[comp, k, at, :]
                if half == 1 and block <= edge + 1:
                    value = value + seam[comp, k, pl.ds(8 * (block - edge), 8), :]
                result[comp, pl.ds(8 * block - RIM, 8), pl.ds(128 * k, 128)] = value * inverse[k, at, :]

    for block in range(max(low, 2), min(high, BLOCKS - 3) + 1):
        new = sweep(work_b, moved, matrix, block)
        if block < first + count:
            final(block, new)
        else:
            for comp in range(2):
                for k in range(2):
                    seam[comp, k, pl.ds(8 * (block - edge), 8), :] = new[comp][k]
        if block + 1 == first + count or (block + 1 - first) % 8 == 0 and block < first + count:
            done = len(moves) // 2
            at = pl.ds(8 * (first + 8 * done) - RIM, 8 * (block + 1 - first - 8 * done))
            for c in range(2):
                moves.append(pltpu.make_async_copy(result.at[c, at], out.at[c, 0, at], sems.at[c, done]))
                moves[-1].start()
    for move in moves:
        move.wait()


def f32(*shape):
    return jax.ShapeDtypeStruct(shape, jnp.float32)


def vmem(*shape):
    return pltpu.VMEM(shape, jnp.float32)


def call(kernel, out_shape, args, mib=6, us=0, **rest):
    return pl.pallas_call(
        kernel,
        out_shape=out_shape,
        compiler_params=pltpu.CompilerParams(vmem_limit_bytes=mib << 20),
        cost_estimate=pl.CostEstimate(flops=us * 1000000, bytes_accessed=us * 3000000, transcendentals=0),
        **rest,
    )(*args)


def local(images, stiffness):
    grid = (3, EXT, 128)
    edge, strip = f32(2 * RIM, TILE), f32(2 * STRIP, 128)
    later_far = send(images, sec_odd)
    later_near = send(images, sec_even)
    in_hbm = pl.BlockSpec(memory_space=pltpu.HBM)
    tile = f32(1, TILE, TILE)
    held = [pltpu.with_memory_space_constraint(x, pltpu.HBM) for x in (images, stiffness)]
    to_o, to_e = call(
        edges_kernel,
        (edge, edge),
        held,
        us=1,
        in_specs=[in_hbm, in_hbm],
        scratch_shapes=[vmem(2 * RIM, TILE), vmem(2 * RIM, TILE), pltpu.SemaphoreType.DMA((2, 2))],
    )
    images, stiffness = call(
        load_kernel,
        (tile, tile),
        (*held, to_o),
        us=1,
        in_specs=[in_hbm, in_hbm, pl.BlockSpec(memory_space=pltpu.VMEM)],
        scratch_shapes=[pltpu.SemaphoreType.DMA((2, CUTS))],
    )
    row_o = send(to_o, row_odd)
    row_e = send(to_e, row_even)

    strip_o, strip_e = call(strip_kernel, (strip, strip), (images, stiffness, row_o, row_e))
    col_o = send(strip_o, col_odd)
    col_e = send(strip_e, col_even)

    band = call(band_kernel, f32(3 * 128, 3 * 128), (to_o,), us=1)

    rims = call(rims_kernel, f32(RIMS, 128), (row_o, row_e, col_o, col_e))
    rims_far = send(rims, sec_odd)
    rims_near = send(rims, sec_even)
    ext, gx, gy, matrix, inverse, known = call(
        matrix_kernel,
        (f32(3, EXT + 16, 128), f32(*grid), f32(*grid), f32(3, *grid), f32(*grid), f32(3, EXT, TILE)),
        (images, stiffness, row_o, row_e, col_o, col_e, band),
        mib=20,
        us=4,
        scratch_shapes=[vmem(*grid), vmem(3, *grid), vmem(3 * EXT, 3 * 128)],
    )
    everywhere = [pl.BlockSpec(memory_space=pltpu.VMEM)] * 5
    tensor, rhs, field, sent_a, sent_b, sent = call(
        first_kernel,
        (f32(5, 1, TILE, TILE), f32(2, *grid), f32(2, *grid), *[f32(rows, 128) for rows in SENT], f32(sum(SENT), 128)),
        (ext, gx, gy, matrix, inverse, known, later_far, later_near, rims_far, rims_near, band),
        mib=20,
        us=5,
        out_specs=[pl.BlockSpec(memory_space=pl.ANY)] + everywhere,
        scratch_shapes=[
            vmem(*grid),
            vmem(2, *grid),
            vmem(2 * EXT, 3 * 128),
            vmem(2, *grid),
            vmem(2, EXT, TILE),
            pltpu.SemaphoreType.DMA((2,)),
        ],
    )

    near = send(sent, sec_even)
    far_a, far_b = send(sent_a, sec_odd), send(sent_b, sec_odd)
    carried = call(
        carry_kernel,
        f32(2, 2, EXT, 128),
        (rhs, matrix, inverse, field, near),
        mib=16,
        us=3,
        scratch_shapes=[vmem(2, *grid), vmem(2, *grid), vmem(2, *grid), vmem(2, 8 * max(COUNTS), 128)],
    )
    whole = pl.BlockSpec(memory_space=pltpu.VMEM)
    anywhere = pl.BlockSpec(memory_space=pl.ANY)
    final = f32(2, 1, TILE, TILE)
    scratch = [
        vmem(2, *grid),
        vmem(2, *grid),
        vmem(2, *grid),
        vmem(2, 8 * max(COUNTS), 128),
        vmem(2, TILE, TILE),
        pltpu.SemaphoreType.DMA((2, CUTS)),
    ]
    field, seam = call(
        functools.partial(second_kernel, 0),
        (final, f32(2, 2, 16, 128)),
        (matrix, inverse, carried, far_a),
        mib=16,
        us=2,
        out_specs=[anywhere, whole],
        scratch_shapes=scratch,
    )
    field = call(
        functools.partial(second_kernel, 1),
        final,
        (matrix, inverse, carried, far_b, seam, field),
        mib=16,
        us=2,
        in_specs=[whole] * 5 + [anywhere],
        out_specs=anywhere,
        input_output_aliases={5: 0},
        scratch_shapes=scratch,
    )
    return tensor, field


def solution(mesh):
    in_specs = (P("sec", "row", "col"), P("sec", "row", "col"))
    out_specs = (P(None, "sec", "row", "col"), P(None, "sec", "row", "col"))
    return jax.shard_map(local, mesh=mesh, in_specs=in_specs, out_specs=out_specs, check_vma=False)
```

```python
import functools

import jax
import jax.numpy as jnp
from jax import lax
from jax.experimental import pallas as pl
from jax.experimental.pallas import tpu as pltpu
from jax.sharding import PartitionSpec as P

RADIUS = 4
COUPLING = 0.25
AXES = ("sec", "row", "col")

TILE = 256
RIM = 16
EXT = TILE + 2 * RIM
BLOCKS = EXT // 8
INNER = BLOCKS - 2
GROUP = 5
FIELD_RIM = 8
COUNTS = (24, INNER - 24)
STARTS = (1, 1 + COUNTS[0])
FOLD = 3
SENT = [32 * count + 16 * FOLD for count in COUNTS]
CUTS = 4
STRIP = GROUP * 8
RIMS = 4 * RIM + 2 * STRIP


def sizes():
    return [lax.axis_size(name) for name in AXES]


def even(i):
    return i ^ 1


def odd(i):
    return ((i + 1) ^ 1) - 1


def send(value, move):
    secs, rows, cols = sizes()
    found = []
    for s in range(secs):
        for r in range(rows):
            for c in range(cols):
                to = move(s, r, c, secs, rows, cols)
                found.append(((s * rows + r) * cols + c, (to[0] * rows + to[1]) * cols + to[2]))
    return lax.ppermute(value, AXES, found)


def row_even(s, r, c, secs, rows, cols):
    return s, even(r), c


def row_odd(s, r, c, secs, rows, cols):
    if 0 < r < rows - 1:
        return s, odd(r), c
    return s, r, even(c)


def col_even(s, r, c, secs, rows, cols):
    return s, r, even(c)


def col_odd(s, r, c, secs, rows, cols):
    if 0 < c < cols - 1:
        return s, r, odd(c)
    return s, even(r), c


def sec_even(s, r, c, secs, rows, cols):
    return even(s), r, c


def sec_odd(s, r, c, secs, rows, cols):
    if 0 < s < secs - 1:
        return odd(s), r, c
    return s, even(r), c


def lanes():
    return lax.broadcasted_iota(jnp.int32, (8, 128), 1)


def from_left(tiles, steps):
    rolled = [pltpu.roll(t, steps, 1) for t in tiles]
    edge = lanes() < steps
    return [jnp.where(edge, rolled[(k + 2) % 3], rolled[k]) for k in range(3)]


def from_right(tiles, steps):
    rolled = [pltpu.roll(t, 128 - steps, 1) for t in tiles]
    edge = lanes() >= 128 - steps
    return [jnp.where(edge, rolled[(k + 1) % 3], rolled[k]) for k in range(3)]


def ext_block(main, top, bottom, block, k):
    cols = pl.ds(128 * k, 128)
    if block < 2:
        return top(8 * block, cols)
    if block >= BLOCKS - 2:
        return bottom(8 * (block - (BLOCKS - 2)), cols)
    return main(8 * (block - 2), cols)


def reader(ref, offset=0):
    return lambda row, cols: ref[pl.ds(offset + row, 8), cols]


def tile_of(ref):
    return lambda row, cols: ref[0, pl.ds(row, 8), cols]


def is_odd(axis):
    return lax.rem(lax.axis_index(axis), 2) == 1


def row_halo(from_o, from_e):
    flag = is_odd("row")
    r = lax.axis_index("row")
    above, below = r > 0, r < lax.axis_size("row") - 1

    def top(row, cols):
        return jnp.where(above, jnp.where(flag, from_e(row, cols), from_o(row, cols)), 0.0)

    def bottom(row, cols):
        return jnp.where(below, jnp.where(flag, from_o(row, cols), from_e(row, cols)), 0.0)

    return top, bottom


def edges_kernel(image, stiff, out_o, out_e, first, last, sems):
    flag = is_odd("row")
    copies = []
    for m, ref in enumerate((image, stiff)):
        for n, (dst, at) in enumerate(((first, 0), (last, TILE - RIM))):
            copies.append(pltpu.make_async_copy(ref.at[0, pl.ds(at, RIM)], dst.at[pl.ds(RIM * m, RIM)], sems.at[m, n]))
    for copy in copies:
        copy.start()
    for copy in copies:
        copy.wait()
    for n in range(2 * RIM // 8):
        rows = pl.ds(8 * n, 8)
        a, b = first[rows, :], last[rows, :]
        out_o[rows, :] = jnp.where(flag, b, a)
        out_e[rows, :] = jnp.where(flag, a, b)


def load_kernel(image, stiff, after, img, stf, sems):
    copies = []
    for n in range(CUTS):
        at = pl.ds(TILE // CUTS * n, TILE // CUTS)
        copies.append(pltpu.make_async_copy(image.at[0, at], img.at[0, at], sems.at[0, n]))
        copies.append(pltpu.make_async_copy(stiff.at[0, at], stf.at[0, at], sems.at[1, n]))
    for copy in copies:
        copy.start()
    for copy in copies:
        copy.wait()


def strip_kernel(image, stiff, row_o, row_e, out_o, out_e):
    col_flag = is_odd("col")
    lane = lanes()
    for n, main in enumerate((image, stiff)):
        top, bottom = row_halo(reader(row_o, RIM * n), reader(row_e, RIM * n))
        left = [jnp.zeros((8, 128), jnp.float32)] * GROUP
        right = [jnp.zeros((8, 128), jnp.float32)] * GROUP
        for block in range(BLOCKS):
            g, place = divmod(block, GROUP)
            here = (lane >= 16 * g) & (lane < 16 * g + 16)
            first = ext_block(tile_of(main), top, bottom, block, 0)
            last = ext_block(tile_of(main), top, bottom, block, 1)
            first = pltpu.roll(first, 16 * g, 1) if g else first
            last = pltpu.roll(last, (16 + 16 * g) % 128, 1) if g != 7 else last
            left[place] = jnp.where(here, first, left[place])
            right[place] = jnp.where(here, last, right[place])
        for place in range(GROUP):
            rows = pl.ds(STRIP * n + 8 * place, 8)
            out_o[rows, :] = jnp.where(col_flag, right[place], left[place])
            out_e[rows, :] = jnp.where(col_flag, left[place], right[place])


def rims_kernel(row_o, row_e, col_o, col_e, out):
    for m, ref in enumerate((row_o, row_e)):
        for k in range(2):
            for n in range(RIM // 8):
                out[pl.ds(RIM * (2 * m + k) + 8 * n, 8), :] = ref[pl.ds(8 * n, 8), pl.ds(128 * k, 128)]
    for m, ref in enumerate((col_o, col_e)):
        for n in range(GROUP):
            out[pl.ds(4 * RIM + STRIP * m + 8 * n, 8), :] = ref[pl.ds(8 * n, 8), :]


def side_block(from_o, from_e, block):
    lane = lanes()
    c = lax.axis_index("col")
    flag = is_odd("col")
    right_ok = (lane < 16) & (c < lax.axis_size("col") - 1)
    left_ok = (lane >= 112) & (c > 0)
    g, place = divmod(block, GROUP)
    cols = pl.ds(0, 128)
    a, b = from_o(8 * place, cols), from_e(8 * place, cols)
    right = jnp.where(flag, a, b)
    left = jnp.where(flag, b, a)
    right = pltpu.roll(right, 128 - 16 * g, 1) if g else right
    left = pltpu.roll(left, (112 - 16 * g) % 128, 1) if g != 7 else left
    return jnp.where(right_ok, right, jnp.where(left_ok, left, 0.0))


def band_kernel(start, band):
    wide = 3 * 128
    for n in range(wide // 8):
        a = lax.broadcasted_iota(jnp.int32, (8, wide), 0) + 8 * n
        b = lax.broadcasted_iota(jnp.int32, (8, wide), 1)
        apart = jnp.abs(a - b)
        near = (apart <= RADIUS) | (apart >= wide - RADIUS)
        band[pl.ds(8 * n, 8), :] = jnp.where(near, 1.0, 0.0)


def spread(prods, band, sums, count):
    ones = band[...].astype(jnp.bfloat16)
    rest = prods[...]
    total = None
    for part in range(3):
        piece = rest.astype(jnp.bfloat16)
        if part < 2:
            rest = rest - piece.astype(jnp.float32)
        found = jnp.dot(piece, ones, preferred_element_type=jnp.float32)
        total = found if total is None else total + found
    for p in range(count):
        for k in range(3):
            sums[p, k] = total[EXT * p : EXT * (p + 1), 128 * k : 128 * (k + 1)]


def tall(ref, p, k, row):
    terms = [ref[p, k, pl.ds(row + d, 8), :] for d in range(-RADIUS, RADIUS + 1)]
    while len(terms) > 1:
        terms = [sum(terms[i : i + 2]) for i in range(0, len(terms), 2)]
    return terms[0]


def mean_scale():
    keep = lax.axis_index("sec") < lax.axis_size("sec") - 1
    return jnp.where(keep, 1.0 / float((2 * RADIUS + 1) ** 2), 0.0)


def matrix_kernel(
    image, stiff, row_o, row_e, col_o, col_e, band,
    ext, gx_out, gy_out, matrix, inverse, tensor,
    wide, sums, prods,
):
    lane = lanes()
    sub = lax.broadcasted_iota(jnp.int32, (8, 128), 0)
    zero = jnp.zeros((8, 128), jnp.float32)
    r, c = lax.axis_index("row"), lax.axis_index("col")
    rows, cols = lax.axis_size("row"), lax.axis_size("col")

    for k in range(3):
        ext[k, pl.ds(0, 8), :] = zero
        ext[k, pl.ds(EXT + 8, 8), :] = zero
    for n, (main, dst, shift) in enumerate(((image, ext, 8), (stiff, wide, 0))):
        top, bottom = row_halo(reader(row_o, RIM * n), reader(row_e, RIM * n))
        side_o, side_e = reader(col_o, STRIP * n), reader(col_e, STRIP * n)
        for block in range(BLOCKS):
            at = pl.ds(8 * block + shift, 8)
            for k in range(3):
                if k < 2:
                    value = ext_block(tile_of(main), top, bottom, block, k)
                else:
                    value = side_block(side_o, side_e, block)
                dst[k, at, :] = jnp.sqrt(value) if n else value

    low = jnp.where(r == 0, RIM, 0)
    high = jnp.where(r == rows - 1, RIM + TILE, EXT)
    col_ok = ((lane < 16) & (c < cols - 1)) | ((lane >= 112) & (c > 0))

    def gradient(block, carry):
        row = pl.multiple_of(8 * block, 8)
        at = pl.ds(row, 8)
        here = sub + row
        row_ok = (here >= low) & (here < high)
        cur = [ext[k, pl.ds(row + 8, 8), :] for k in range(3)]
        left = from_left(cur, 1)
        right = from_right(cur, 1)
        gx, gy = [], []
        for k in range(3):
            ok = row_ok & col_ok if k == 2 else row_ok
            gx.append(jnp.where(ok, (right[k] - left[k]) * 0.5, 0.0))
            gy.append(jnp.where(ok, (ext[k, pl.ds(row + 9, 8), :] - ext[k, pl.ds(row + 7, 8), :]) * 0.5, 0.0))
            gx_out[k, at, :] = gx[k]
            gy_out[k, at, :] = gy[k]
        for p, (a, b) in enumerate(((gx, gx), (gx, gy), (gy, gy))):
            rows_at = pl.ds(pl.multiple_of(EXT * p + row, 8), 8)
            for k in range(3):
                prods[rows_at, pl.ds(128 * k, 128)] = a[k] * b[k]
        return carry

    lax.fori_loop(0, BLOCKS, gradient, 0, unroll=12)
    spread(prods, band, sums, 3)
    scale = mean_scale()

    def system(block, carry):
        row = pl.multiple_of(8 * block, 8)
        at = pl.ds(row, 8)
        cur = [wide[k, at, :] for k in range(3)]
        left = from_left(cur, 1)
        right = from_right(cur, 1)
        for k in range(3):
            xx, xy, yy = (tall(sums, p, k, row) * scale for p in range(3))
            if k < 2:
                for p, value in enumerate((xx, xy, yy)):
                    tensor[p, at, pl.ds(128 * k, 128)] = value
            q = cur[k]
            around = (wide[k, pl.ds(row - 1, 8), :] + wide[k, pl.ds(row + 1, 8), :]) + (left[k] + right[k])
            diag = q * around + 2.0 * COUPLING
            first, second = xx + diag, yy + diag
            over = (q * q) / (first * second - xy * xy)
            matrix[0, k, at, :] = second * over
            matrix[1, k, at, :] = xy * over
            matrix[2, k, at, :] = first * over
            inverse[k, at, :] = jnp.where(q > 0.0, 1.0 / q, 0.0)
        return carry

    lax.fori_loop(1, BLOCKS - 1, system, 0, unroll=INNER)


def clear_rims(ref):
    zero = jnp.zeros((8, 128), jnp.float32)
    for comp in range(2):
        for k in range(3):
            ref[comp, k, pl.ds(0, 8), :] = zero
            ref[comp, k, pl.ds(EXT - 8, 8), :] = zero


def sweep(g, rhs, matrix, block):
    row = pl.multiple_of(8 * block, 8)
    here = pl.ds(row, 8)
    sums = []
    for comp in range(2):
        cur = [g[comp, k, here, :] for k in range(3)]
        up = [g[comp, k, pl.ds(row - 1, 8), :] for k in range(3)]
        down = [g[comp, k, pl.ds(row + 1, 8), :] for k in range(3)]
        left = from_left(cur, 1)
        right = from_right(cur, 1)
        sums.append([(up[k] + down[k]) + (left[k] + right[k]) for k in range(3)])
    first, second = [], []
    for k in range(3):
        a, b, d = (matrix[i, k, here, :] for i in range(3))
        first.append(rhs[0, k, here, :] + (a * sums[0][k] - b * sums[1][k]))
        second.append(rhs[1, k, here, :] + (d * sums[1][k] - b * sums[0][k]))
    return first, second


def step(src, dst, rhs, matrix, low=1, high=BLOCKS - 2, unroll=INNER // 2):
    def body(block, carry):
        new = sweep(src, rhs, matrix, block)
        at = pl.ds(pl.multiple_of(8 * block, 8), 8)
        for comp in range(2):
            for k in range(3):
                dst[comp, k, at, :] = new[comp][k]
        return carry

    lax.fori_loop(low, high + 1, body, 0, unroll=unroll)


def first_kernel(
    ext, gx, gy, matrix, inverse, later_far, later_near, far, near, band,
    fresh, rhs, field, work, done, sent,
    chg, sums, prods,
):
    s, secs = lax.axis_index("sec"), lax.axis_size("sec")
    use_far, use_near = lax.rem(s, 2) == 1, s < secs - 1

    def pick(a, b):
        return jnp.where(use_near, jnp.where(use_far, a, b), 0.0)

    def rim_rows(base):
        def read(row, cols):
            at = pl.ds(base + RIM * (cols.start // 128) + row, 8)
            return pick(far[at, :], near[at, :])

        return read

    def rim_cols(base):
        def read(row, cols):
            at = pl.ds(base + row, 8)
            return pick(far[at, :], near[at, :])

        return read

    def main(row, cols):
        at = pl.ds(row, 8)
        return pick(later_far[0, at, cols], later_near[0, at, cols])

    top, bottom = row_halo(rim_rows(0), rim_rows(2 * RIM))
    side_o, side_e = rim_cols(4 * RIM), rim_cols(4 * RIM + STRIP)
    for block in range(BLOCKS):
        at = pl.ds(8 * block, 8)
        old = pl.ds(8 * block + 8, 8)
        for k in range(2):
            chg[k, at, :] = ext_block(main, top, bottom, block, k) - ext[k, old, :]
        chg[2, at, :] = side_block(side_o, side_e, block) - ext[2, old, :]

    def products(block, carry):
        row = pl.multiple_of(8 * block, 8)
        at = pl.ds(row, 8)
        for p, grad in enumerate((gx, gy)):
            rows_at = pl.ds(pl.multiple_of(EXT * p + row, 8), 8)
            for k in range(3):
                prods[rows_at, pl.ds(128 * k, 128)] = grad[k, at, :] * chg[k, at, :]
        return carry

    lax.fori_loop(0, BLOCKS, products, 0, unroll=6)
    spread(prods, band, sums, 2)
    scale = mean_scale()
    clear_rims(field)
    clear_rims(work)

    def right_side(block, carry):
        row = pl.multiple_of(8 * block, 8)
        at = pl.ds(row, 8)
        for k in range(3):
            xt, yt = (tall(sums, p, k, row) * scale for p in range(2))
            if k < 2:
                fresh[0, at, pl.ds(128 * k, 128)] = xt
                fresh[1, at, pl.ds(128 * k, 128)] = yt
            a, b, d = (matrix[i, k, at, :] for i in range(3))
            inv = inverse[k, at, :]
            rx = (b * yt - a * xt) * inv
            ry = (b * xt - d * yt) * inv
            rhs[0, k, at, :] = rx
            rhs[1, k, at, :] = ry
            work[0, k, at, :] = rx
            work[1, k, at, :] = ry
        return carry

    lax.fori_loop(1, BLOCKS - 1, right_side, 0, unroll=INNER)
    edge = COUNTS[0]
    step(work, field, rhs, matrix, 1, edge + 4, edge // 2 + 2)
    step(field, work, rhs, matrix, 1, edge + 2, edge // 2 + 1)
    send_part(0, work, done, sent, rhs, matrix, inverse)


def send_part(half, src, dst, sent, rhs, matrix, inverse):
    lane = lanes()
    start, count = STARTS[half], COUNTS[half]

    def last(block, carry):
        new = sweep(src, rhs, matrix, block)
        at = pl.ds(pl.multiple_of(8 * block, 8), 8)
        for comp in range(2):
            for k in range(3):
                dst[comp, k, at, :] = new[comp][k]
            for k in range(2):
                to = pl.multiple_of(8 * ((2 * comp + k) * count + block - start), 8)
                sent[pl.ds(to, 8), :] = new[comp][k] * inverse[k, at, :]
        return carry

    lax.fori_loop(start, start + count, last, 0, unroll=count)

    for comp in range(2):
        strip = [jnp.zeros((8, 128), jnp.float32)] * FOLD
        for n in range(count):
            g, place = divmod(n, FOLD)
            at = pl.ds(8 * (start + n), 8)
            tile = pltpu.roll(dst[comp, 2, at, :] * inverse[2, at, :], FIELD_RIM + 16 * g, 1)
            strip[place] = jnp.where((lane >= 16 * g) & (lane < 16 * g + 16), tile, strip[place])
        for place in range(FOLD):
            sent[pl.ds(32 * count + 8 * (FOLD * comp + place), 8), :] = strip[place]


def tail_kernel(rhs, matrix, inverse, once, twice, done, after, field, sent, second, third):
    edge = COUNTS[0]
    for ref in (second, third, field):
        clear_rims(ref)
    for comp in range(2):
        for k in range(3):
            for dst, src, low in ((second, twice, edge + 2), (third, once, edge)):
                for block in range(low, low + 3):
                    at = pl.ds(8 * block, 8)
                    dst[comp, k, at, :] = src[comp, k, at, :]
            for block in range(1, edge + 1):
                at = pl.ds(8 * block, 8)
                field[comp, k, at, :] = done[comp, k, at, :]
    step(once, second, rhs, matrix, edge + 5, INNER, INNER - edge - 4)
    step(second, third, rhs, matrix, edge + 3, INNER, INNER - edge - 2)
    send_part(1, third, field, sent, rhs, matrix, inverse)


def beside_terms(half, received, matrix, inverse, strips, store, ok=None):
    lane = lanes()
    start, count = STARTS[half], COUNTS[half]

    def read(at):
        return received[at, :] if ok is None else jnp.where(ok, received[at, :], 0.0)

    for comp in range(2):
        for n in range(count):
            g, place = divmod(n, FOLD)
            tile = read(pl.ds(32 * count + 8 * (FOLD * comp + place), 8))
            tile = pltpu.roll(tile, 128 - FIELD_RIM - 16 * g, 1)
            strips[comp, pl.ds(8 * n, 8), :] = jnp.where((lane < FIELD_RIM) | (lane >= 128 - FIELD_RIM), tile, 0.0)

    def body(n, carry):
        at = pl.ds(pl.multiple_of(8 * (start + n), 8), 8)
        for k in range(3):
            pair = []
            for comp in range(2):
                if k < 2:
                    value = read(pl.ds(pl.multiple_of(8 * ((2 * comp + k) * count + n), 8), 8))
                else:
                    value = strips[comp, pl.ds(pl.multiple_of(8 * n, 8), 8), :]
                pair.append(value * (inverse[k, at, :] * COUPLING))
            a, b, d = (matrix[i, k, at, :] for i in range(3))
            store(k, at, a * pair[0] - b * pair[1], d * pair[1] - b * pair[0])
        return carry

    lax.fori_loop(0, count, body, 0, unroll=count)


def carry_kernel(
    rhs, matrix, inverse, field, near_a, near_b, known, fresh,
    out, tensor,
    moved, work_a, work_b, strips, sems,
):
    inner = pl.ds(RIM, TILE)
    copies = [
        pltpu.make_async_copy(src.at[p, inner], tensor.at[base + p, 0], sems.at[base + p])
        for src, base, count in ((known, 0, 3), (fresh, 3, 2))
        for p in range(count)
    ]
    for copy in copies:
        copy.start()
    clear_rims(work_a)
    clear_rims(work_b)

    def store(k, at, x, y):
        moved[0, k, at, :] = rhs[0, k, at, :] + x
        moved[1, k, at, :] = rhs[1, k, at, :] + y

    for half, near in enumerate((near_a, near_b)):
        beside_terms(half, near, matrix, inverse, strips, store)
    step(field, work_a, moved, matrix)
    step(work_a, work_b, moved, matrix)
    step(work_b, work_a, moved, matrix)

    def last(block, carry):
        new = sweep(work_a, moved, matrix, block)
        at = pl.ds(pl.multiple_of(8 * block, 8), 8)
        for comp in range(2):
            for k in range(2):
                out[comp, k, at, :] = new[comp][k]
        return carry

    lax.fori_loop(2, BLOCKS - 2, last, 0, unroll=16)
    for copy in copies:
        copy.wait()


def second_kernel(half, matrix, inverse, carried, far, *rest):
    if half == 0:
        out, seam, moved, work_a, work_b, strips, result, sems = rest
    else:
        seam, _, out, moved, work_a, work_b, strips, result, sems = rest
    s = lax.axis_index("sec")
    inside = (s > 0) & (s < lax.axis_size("sec") - 1)
    edge = COUNTS[0]
    low, high = (1, edge + 1) if half == 0 else (edge, INNER)
    zero = jnp.zeros((8, 128), jnp.float32)
    for comp in range(2):
        for k in range(3):
            for ref in (moved, work_a, work_b):
                ref[comp, k, pl.ds(8 * low - 8, 8), :] = zero
                ref[comp, k, pl.ds(8 * high + 8, 8), :] = zero
            moved[comp, k, pl.ds(8 * (high if half == 0 else low), 8), :] = zero

    def store(k, at, x, y):
        moved[0, k, at, :] = x
        moved[1, k, at, :] = y

    beside_terms(half, far, matrix, inverse, strips, store, inside)
    step(moved, work_a, moved, matrix, low, high, high + 1 - low)
    step(work_a, work_b, moved, matrix, low, high, high + 1 - low)

    first, count = (2, edge - 2) if half == 0 else (edge, INNER - edge)
    moves = []

    def final(block, new):
        at = pl.ds(8 * block, 8)
        for comp in range(2):
            for k in range(2):
                value = new[comp][k] + carried[comp, k, at, :]
                if half == 1 and block <= edge + 1:
                    value = value + seam[comp, k, pl.ds(8 * (block - edge), 8), :]
                result[comp, pl.ds(8 * block - RIM, 8), pl.ds(128 * k, 128)] = value * inverse[k, at, :]

    for block in range(max(low, 2), min(high, BLOCKS - 3) + 1):
        new = sweep(work_b, moved, matrix, block)
        if block < first + count:
            final(block, new)
        else:
            for comp in range(2):
                for k in range(2):
                    seam[comp, k, pl.ds(8 * (block - edge), 8), :] = new[comp][k]
        if block + 1 == first + count or (block + 1 - first) % 8 == 0 and block < first + count:
            done = len(moves) // 2
            at = pl.ds(8 * (first + 8 * done) - RIM, 8 * (block + 1 - first - 8 * done))
            for c in range(2):
                moves.append(pltpu.make_async_copy(result.at[c, at], out.at[c, 0, at], sems.at[c, done]))
                moves[-1].start()
    for move in moves:
        move.wait()


def f32(*shape):
    return jax.ShapeDtypeStruct(shape, jnp.float32)


def vmem(*shape):
    return pltpu.VMEM(shape, jnp.float32)


def call(kernel, out_shape, args, mib=6, us=0, **rest):
    return pl.pallas_call(
        kernel,
        out_shape=out_shape,
        compiler_params=pltpu.CompilerParams(vmem_limit_bytes=mib << 20),
        cost_estimate=pl.CostEstimate(flops=us * 1000000, bytes_accessed=us * 3000000, transcendentals=0),
        **rest,
    )(*args)


def local(images, stiffness):
    grid = (3, EXT, 128)
    edge, strip = f32(2 * RIM, TILE), f32(2 * STRIP, 128)
    later_far = send(images, sec_odd)
    later_near = send(images, sec_even)
    in_hbm = pl.BlockSpec(memory_space=pltpu.HBM)
    tile = f32(1, TILE, TILE)
    held = [pltpu.with_memory_space_constraint(x, pltpu.HBM) for x in (images, stiffness)]
    to_o, to_e = call(
        edges_kernel,
        (edge, edge),
        held,
        us=1,
        in_specs=[in_hbm, in_hbm],
        scratch_shapes=[vmem(2 * RIM, TILE), vmem(2 * RIM, TILE), pltpu.SemaphoreType.DMA((2, 2))],
    )
    images, stiffness = call(
        load_kernel,
        (tile, tile),
        (*held, to_o),
        us=1,
        in_specs=[in_hbm, in_hbm, pl.BlockSpec(memory_space=pltpu.VMEM)],
        scratch_shapes=[pltpu.SemaphoreType.DMA((2, CUTS))],
    )
    row_o = send(to_o, row_odd)
    row_e = send(to_e, row_even)

    strip_o, strip_e = call(strip_kernel, (strip, strip), (images, stiffness, row_o, row_e))
    col_o = send(strip_o, col_odd)
    col_e = send(strip_e, col_even)

    band = call(band_kernel, f32(3 * 128, 3 * 128), (to_o,), us=1)

    rims = call(rims_kernel, f32(RIMS, 128), (row_o, row_e, col_o, col_e))
    rims_far = send(rims, sec_odd)
    rims_near = send(rims, sec_even)
    ext, gx, gy, matrix, inverse, known = call(
        matrix_kernel,
        (f32(3, EXT + 16, 128), f32(*grid), f32(*grid), f32(3, *grid), f32(*grid), f32(3, EXT, TILE)),
        (images, stiffness, row_o, row_e, col_o, col_e, band),
        mib=20,
        us=4,
        scratch_shapes=[vmem(*grid), vmem(3, *grid), vmem(3 * EXT, 3 * 128)],
    )
    fresh, rhs, twice, once, done, sent_a = call(
        first_kernel,
        (f32(2, EXT, TILE), *[f32(2, *grid)] * 4, f32(SENT[0], 128)),
        (ext, gx, gy, matrix, inverse, later_far, later_near, rims_far, rims_near, band),
        mib=20,
        us=5,
        scratch_shapes=[vmem(*grid), vmem(2, *grid), vmem(2 * EXT, 3 * 128)],
    )

    far_a = send(sent_a, sec_odd)
    near_a = send(sent_a, sec_even)
    field, sent_b = call(
        tail_kernel,
        (f32(2, *grid), f32(SENT[1], 128)),
        (rhs, matrix, inverse, once, twice, done, near_a),
        mib=16,
        us=1,
        scratch_shapes=[vmem(2, *grid), vmem(2, *grid)],
    )
    far_b = send(sent_b, sec_odd)
    near_b = send(sent_b, sec_even)
    whole = pl.BlockSpec(memory_space=pltpu.VMEM)
    anywhere = pl.BlockSpec(memory_space=pl.ANY)
    carried, tensor = call(
        carry_kernel,
        (f32(2, 2, EXT, 128), f32(5, 1, TILE, TILE)),
        (rhs, matrix, inverse, field, near_a, near_b, known, fresh),
        mib=16,
        us=3,
        out_specs=[whole, anywhere],
        scratch_shapes=[
            vmem(2, *grid),
            vmem(2, *grid),
            vmem(2, *grid),
            vmem(2, 8 * max(COUNTS), 128),
            pltpu.SemaphoreType.DMA((5,)),
        ],
    )
    final = f32(2, 1, TILE, TILE)
    scratch = [
        vmem(2, *grid),
        vmem(2, *grid),
        vmem(2, *grid),
        vmem(2, 8 * max(COUNTS), 128),
        vmem(2, TILE, TILE),
        pltpu.SemaphoreType.DMA((2, CUTS)),
    ]
    field, seam = call(
        functools.partial(second_kernel, 0),
        (final, f32(2, 2, 16, 128)),
        (matrix, inverse, carried, far_a),
        mib=16,
        us=2,
        out_specs=[anywhere, whole],
        scratch_shapes=scratch,
    )
    field = call(
        functools.partial(second_kernel, 1),
        final,
        (matrix, inverse, carried, far_b, seam, field),
        mib=16,
        us=2,
        in_specs=[whole] * 5 + [anywhere],
        out_specs=anywhere,
        input_output_aliases={5: 0},
        scratch_shapes=scratch,
    )
    return tensor, field


def solution(mesh):
    in_specs = (P("sec", "row", "col"), P("sec", "row", "col"))
    out_specs = (P(None, "sec", "row", "col"), P(None, "sec", "row", "col"))
    return jax.shard_map(local, mesh=mesh, in_specs=in_specs, out_specs=out_specs, check_vma=False)
```

```python
import functools

import jax
import jax.numpy as jnp
from jax import lax
from jax.experimental import pallas as pl
from jax.experimental.pallas import tpu as pltpu
from jax.sharding import PartitionSpec as P

RADIUS = 4
COUPLING = 0.25
AXES = ("sec", "row", "col")

TILE = 256
RIM = 16
EXT = TILE + 2 * RIM
BLOCKS = EXT // 8
INNER = BLOCKS - 2
GROUP = 5
FIELD_RIM = 8
COUNTS = (20, INNER - 20)
STARTS = (1, 1 + COUNTS[0])
FOLD = 3
SENT = [32 * count + 16 * FOLD for count in COUNTS]
CUTS = 4
STRIP = GROUP * 8
RIMS = 4 * RIM + 2 * STRIP


def sizes():
    return [lax.axis_size(name) for name in AXES]


def even(i):
    return i ^ 1


def odd(i):
    return ((i + 1) ^ 1) - 1


def send(value, move):
    secs, rows, cols = sizes()
    found = []
    for s in range(secs):
        for r in range(rows):
            for c in range(cols):
                to = move(s, r, c, secs, rows, cols)
                found.append(((s * rows + r) * cols + c, (to[0] * rows + to[1]) * cols + to[2]))
    return lax.ppermute(value, AXES, found)


def row_even(s, r, c, secs, rows, cols):
    return s, even(r), c


def row_odd(s, r, c, secs, rows, cols):
    if 0 < r < rows - 1:
        return s, odd(r), c
    return s, r, even(c)


def col_even(s, r, c, secs, rows, cols):
    return s, r, even(c)


def col_odd(s, r, c, secs, rows, cols):
    if 0 < c < cols - 1:
        return s, r, odd(c)
    return s, even(r), c


def sec_even(s, r, c, secs, rows, cols):
    return even(s), r, c


def sec_odd(s, r, c, secs, rows, cols):
    if 0 < s < secs - 1:
        return odd(s), r, c
    return s, even(r), c


def lanes():
    return lax.broadcasted_iota(jnp.int32, (8, 128), 1)


def from_left(tiles, steps):
    rolled = [pltpu.roll(t, steps, 1) for t in tiles]
    edge = lanes() < steps
    return [jnp.where(edge, rolled[(k + 2) % 3], rolled[k]) for k in range(3)]


def from_right(tiles, steps):
    rolled = [pltpu.roll(t, 128 - steps, 1) for t in tiles]
    edge = lanes() >= 128 - steps
    return [jnp.where(edge, rolled[(k + 1) % 3], rolled[k]) for k in range(3)]


def ext_block(main, top, bottom, block, k):
    cols = pl.ds(128 * k, 128)
    if block < 2:
        return top(8 * block, cols)
    if block >= BLOCKS - 2:
        return bottom(8 * (block - (BLOCKS - 2)), cols)
    return main(8 * (block - 2), cols)


def reader(ref, offset=0):
    return lambda row, cols: ref[pl.ds(offset + row, 8), cols]


def tile_of(ref):
    return lambda row, cols: ref[0, pl.ds(row, 8), cols]


def is_odd(axis):
    return lax.rem(lax.axis_index(axis), 2) == 1


def row_halo(from_o, from_e):
    flag = is_odd("row")
    r = lax.axis_index("row")
    above, below = r > 0, r < lax.axis_size("row") - 1

    def top(row, cols):
        return jnp.where(above, jnp.where(flag, from_e(row, cols), from_o(row, cols)), 0.0)

    def bottom(row, cols):
        return jnp.where(below, jnp.where(flag, from_o(row, cols), from_e(row, cols)), 0.0)

    return top, bottom


def edges_kernel(image, stiff, out_o, out_e, first, last, sems):
    flag = is_odd("row")
    copies = []
    for m, ref in enumerate((image, stiff)):
        for n, (dst, at) in enumerate(((first, 0), (last, TILE - RIM))):
            copies.append(pltpu.make_async_copy(ref.at[0, pl.ds(at, RIM)], dst.at[pl.ds(RIM * m, RIM)], sems.at[m, n]))
    for copy in copies:
        copy.start()
    for copy in copies:
        copy.wait()
    for n in range(2 * RIM // 8):
        rows = pl.ds(8 * n, 8)
        a, b = first[rows, :], last[rows, :]
        out_o[rows, :] = jnp.where(flag, b, a)
        out_e[rows, :] = jnp.where(flag, a, b)


def load_kernel(image, stiff, after, img, stf, sems):
    copies = []
    for n in range(CUTS):
        at = pl.ds(TILE // CUTS * n, TILE // CUTS)
        copies.append(pltpu.make_async_copy(image.at[0, at], img.at[0, at], sems.at[0, n]))
        copies.append(pltpu.make_async_copy(stiff.at[0, at], stf.at[0, at], sems.at[1, n]))
    for copy in copies:
        copy.start()
    for copy in copies:
        copy.wait()


def strip_kernel(image, stiff, row_o, row_e, out_o, out_e):
    col_flag = is_odd("col")
    lane = lanes()
    for n, main in enumerate((image, stiff)):
        top, bottom = row_halo(reader(row_o, RIM * n), reader(row_e, RIM * n))
        left = [jnp.zeros((8, 128), jnp.float32)] * GROUP
        right = [jnp.zeros((8, 128), jnp.float32)] * GROUP
        for block in range(BLOCKS):
            g, place = divmod(block, GROUP)
            here = (lane >= 16 * g) & (lane < 16 * g + 16)
            first = ext_block(tile_of(main), top, bottom, block, 0)
            last = ext_block(tile_of(main), top, bottom, block, 1)
            first = pltpu.roll(first, 16 * g, 1) if g else first
            last = pltpu.roll(last, (16 + 16 * g) % 128, 1) if g != 7 else last
            left[place] = jnp.where(here, first, left[place])
            right[place] = jnp.where(here, last, right[place])
        for place in range(GROUP):
            rows = pl.ds(STRIP * n + 8 * place, 8)
            out_o[rows, :] = jnp.where(col_flag, right[place], left[place])
            out_e[rows, :] = jnp.where(col_flag, left[place], right[place])


def rims_kernel(row_o, row_e, col_o, col_e, out):
    for m, ref in enumerate((row_o, row_e)):
        for k in range(2):
            for n in range(RIM // 8):
                out[pl.ds(RIM * (2 * m + k) + 8 * n, 8), :] = ref[pl.ds(8 * n, 8), pl.ds(128 * k, 128)]
    for m, ref in enumerate((col_o, col_e)):
        for n in range(GROUP):
            out[pl.ds(4 * RIM + STRIP * m + 8 * n, 8), :] = ref[pl.ds(8 * n, 8), :]


def side_block(from_o, from_e, block):
    lane = lanes()
    c = lax.axis_index("col")
    flag = is_odd("col")
    right_ok = (lane < 16) & (c < lax.axis_size("col") - 1)
    left_ok = (lane >= 112) & (c > 0)
    g, place = divmod(block, GROUP)
    cols = pl.ds(0, 128)
    a, b = from_o(8 * place, cols), from_e(8 * place, cols)
    right = jnp.where(flag, a, b)
    left = jnp.where(flag, b, a)
    right = pltpu.roll(right, 128 - 16 * g, 1) if g else right
    left = pltpu.roll(left, (112 - 16 * g) % 128, 1) if g != 7 else left
    return jnp.where(right_ok, right, jnp.where(left_ok, left, 0.0))


def band_kernel(start, band):
    wide = 3 * 128
    for n in range(wide // 8):
        a = lax.broadcasted_iota(jnp.int32, (8, wide), 0) + 8 * n
        b = lax.broadcasted_iota(jnp.int32, (8, wide), 1)
        apart = jnp.abs(a - b)
        near = (apart <= RADIUS) | (apart >= wide - RADIUS)
        band[pl.ds(8 * n, 8), :] = jnp.where(near, 1.0, 0.0)


def spread(prods, band, sums, count):
    ones = band[...].astype(jnp.bfloat16)
    rest = prods[...]
    total = None
    for part in range(3):
        piece = rest.astype(jnp.bfloat16)
        if part < 2:
            rest = rest - piece.astype(jnp.float32)
        found = jnp.dot(piece, ones, preferred_element_type=jnp.float32)
        total = found if total is None else total + found
    for p in range(count):
        for k in range(3):
            sums[p, k] = total[EXT * p : EXT * (p + 1), 128 * k : 128 * (k + 1)]


def tall(ref, p, k, row):
    terms = [ref[p, k, pl.ds(row + d, 8), :] for d in range(-RADIUS, RADIUS + 1)]
    while len(terms) > 1:
        terms = [sum(terms[i : i + 2]) for i in range(0, len(terms), 2)]
    return terms[0]


def mean_scale():
    keep = lax.axis_index("sec") < lax.axis_size("sec") - 1
    return jnp.where(keep, 1.0 / float((2 * RADIUS + 1) ** 2), 0.0)


def matrix_kernel(
    image, stiff, row_o, row_e, col_o, col_e, band,
    ext, gx_out, gy_out, matrix, inverse, tensor,
    wide, sums, prods,
):
    lane = lanes()
    sub = lax.broadcasted_iota(jnp.int32, (8, 128), 0)
    zero = jnp.zeros((8, 128), jnp.float32)
    r, c = lax.axis_index("row"), lax.axis_index("col")
    rows, cols = lax.axis_size("row"), lax.axis_size("col")

    for k in range(3):
        ext[k, pl.ds(0, 8), :] = zero
        ext[k, pl.ds(EXT + 8, 8), :] = zero
    for n, (main, dst, shift) in enumerate(((image, ext, 8), (stiff, wide, 0))):
        top, bottom = row_halo(reader(row_o, RIM * n), reader(row_e, RIM * n))
        side_o, side_e = reader(col_o, STRIP * n), reader(col_e, STRIP * n)
        for block in range(BLOCKS):
            at = pl.ds(8 * block + shift, 8)
            for k in range(3):
                if k < 2:
                    value = ext_block(tile_of(main), top, bottom, block, k)
                else:
                    value = side_block(side_o, side_e, block)
                dst[k, at, :] = jnp.sqrt(value) if n else value

    low = jnp.where(r == 0, RIM, 0)
    high = jnp.where(r == rows - 1, RIM + TILE, EXT)
    col_ok = ((lane < 16) & (c < cols - 1)) | ((lane >= 112) & (c > 0))

    def gradient(block, carry):
        row = pl.multiple_of(8 * block, 8)
        at = pl.ds(row, 8)
        here = sub + row
        row_ok = (here >= low) & (here < high)
        cur = [ext[k, pl.ds(row + 8, 8), :] for k in range(3)]
        left = from_left(cur, 1)
        right = from_right(cur, 1)
        gx, gy = [], []
        for k in range(3):
            ok = row_ok & col_ok if k == 2 else row_ok
            gx.append(jnp.where(ok, (right[k] - left[k]) * 0.5, 0.0))
            gy.append(jnp.where(ok, (ext[k, pl.ds(row + 9, 8), :] - ext[k, pl.ds(row + 7, 8), :]) * 0.5, 0.0))
            gx_out[k, at, :] = gx[k]
            gy_out[k, at, :] = gy[k]
        for p, (a, b) in enumerate(((gx, gx), (gx, gy), (gy, gy))):
            rows_at = pl.ds(pl.multiple_of(EXT * p + row, 8), 8)
            for k in range(3):
                prods[rows_at, pl.ds(128 * k, 128)] = a[k] * b[k]
        return carry

    lax.fori_loop(0, BLOCKS, gradient, 0, unroll=18)
    spread(prods, band, sums, 3)
    scale = mean_scale()

    def system(block, carry):
        row = pl.multiple_of(8 * block, 8)
        at = pl.ds(row, 8)
        cur = [wide[k, at, :] for k in range(3)]
        left = from_left(cur, 1)
        right = from_right(cur, 1)
        for k in range(3):
            xx, xy, yy = (tall(sums, p, k, row) * scale for p in range(3))
            if k < 2:
                for p, value in enumerate((xx, xy, yy)):
                    tensor[p, at, pl.ds(128 * k, 128)] = value
            q = cur[k]
            around = (wide[k, pl.ds(row - 1, 8), :] + wide[k, pl.ds(row + 1, 8), :]) + (left[k] + right[k])
            diag = q * around + 2.0 * COUPLING
            first, second = xx + diag, yy + diag
            over = (q * q) / (first * second - xy * xy)
            matrix[0, k, at, :] = second * over
            matrix[1, k, at, :] = xy * over
            matrix[2, k, at, :] = first * over
            inverse[k, at, :] = jnp.where(q > 0.0, 1.0 / q, 0.0)
        return carry

    lax.fori_loop(1, BLOCKS - 1, system, 0, unroll=INNER)


def clear_rims(ref):
    zero = jnp.zeros((8, 128), jnp.float32)
    for comp in range(2):
        for k in range(3):
            ref[comp, k, pl.ds(0, 8), :] = zero
            ref[comp, k, pl.ds(EXT - 8, 8), :] = zero


def sweep(g, rhs, matrix, block):
    row = pl.multiple_of(8 * block, 8)
    here = pl.ds(row, 8)
    sums = []
    for comp in range(2):
        cur = [g[comp, k, here, :] for k in range(3)]
        up = [g[comp, k, pl.ds(row - 1, 8), :] for k in range(3)]
        down = [g[comp, k, pl.ds(row + 1, 8), :] for k in range(3)]
        left = from_left(cur, 1)
        right = from_right(cur, 1)
        sums.append([(up[k] + down[k]) + (left[k] + right[k]) for k in range(3)])
    first, second = [], []
    for k in range(3):
        a, b, d = (matrix[i, k, here, :] for i in range(3))
        first.append(rhs[0, k, here, :] + (a * sums[0][k] - b * sums[1][k]))
        second.append(rhs[1, k, here, :] + (d * sums[1][k] - b * sums[0][k]))
    return first, second


def step(src, dst, rhs, matrix, low=1, high=BLOCKS - 2, unroll=INNER // 2):
    def body(block, carry):
        new = sweep(src, rhs, matrix, block)
        at = pl.ds(pl.multiple_of(8 * block, 8), 8)
        for comp in range(2):
            for k in range(3):
                dst[comp, k, at, :] = new[comp][k]
        return carry

    lax.fori_loop(low, high + 1, body, 0, unroll=unroll)


def first_kernel(
    ext, gx, gy, matrix, inverse, later_far, later_near, far, near, band,
    fresh, rhs, field, work, done, sent,
    chg, sums, prods,
):
    s, secs = lax.axis_index("sec"), lax.axis_size("sec")
    use_far, use_near = lax.rem(s, 2) == 1, s < secs - 1

    def pick(a, b):
        return jnp.where(use_near, jnp.where(use_far, a, b), 0.0)

    def rim_rows(base):
        def read(row, cols):
            at = pl.ds(base + RIM * (cols.start // 128) + row, 8)
            return pick(far[at, :], near[at, :])

        return read

    def rim_cols(base):
        def read(row, cols):
            at = pl.ds(base + row, 8)
            return pick(far[at, :], near[at, :])

        return read

    def main(row, cols):
        at = pl.ds(row, 8)
        return pick(later_far[0, at, cols], later_near[0, at, cols])

    top, bottom = row_halo(rim_rows(0), rim_rows(2 * RIM))
    side_o, side_e = rim_cols(4 * RIM), rim_cols(4 * RIM + STRIP)
    for block in range(BLOCKS):
        at = pl.ds(8 * block, 8)
        old = pl.ds(8 * block + 8, 8)
        for k in range(2):
            chg[k, at, :] = ext_block(main, top, bottom, block, k) - ext[k, old, :]
        chg[2, at, :] = side_block(side_o, side_e, block) - ext[2, old, :]

    def products(block, carry):
        row = pl.multiple_of(8 * block, 8)
        at = pl.ds(row, 8)
        for p, grad in enumerate((gx, gy)):
            rows_at = pl.ds(pl.multiple_of(EXT * p + row, 8), 8)
            for k in range(3):
                prods[rows_at, pl.ds(128 * k, 128)] = grad[k, at, :] * chg[k, at, :]
        return carry

    lax.fori_loop(0, BLOCKS, products, 0, unroll=12)
    spread(prods, band, sums, 2)
    scale = mean_scale()
    clear_rims(field)
    clear_rims(work)

    def right_side(block, carry):
        row = pl.multiple_of(8 * block, 8)
        at = pl.ds(row, 8)
        for k in range(3):
            xt, yt = (tall(sums, p, k, row) * scale for p in range(2))
            if k < 2:
                fresh[0, at, pl.ds(128 * k, 128)] = xt
                fresh[1, at, pl.ds(128 * k, 128)] = yt
            a, b, d = (matrix[i, k, at, :] for i in range(3))
            inv = inverse[k, at, :]
            rx = (b * yt - a * xt) * inv
            ry = (b * xt - d * yt) * inv
            rhs[0, k, at, :] = rx
            rhs[1, k, at, :] = ry
            work[0, k, at, :] = rx
            work[1, k, at, :] = ry
        return carry

    lax.fori_loop(1, BLOCKS - 1, right_side, 0, unroll=INNER)
    edge = COUNTS[0]
    step(work, field, rhs, matrix, 1, edge + 4, edge // 2 + 2)
    step(field, work, rhs, matrix, 1, edge + 2, edge // 2 + 1)
    send_part(0, work, done, sent, rhs, matrix, inverse)


def send_part(half, src, dst, sent, rhs, matrix, inverse):
    lane = lanes()
    start, count = STARTS[half], COUNTS[half]

    def last(block, carry):
        new = sweep(src, rhs, matrix, block)
        at = pl.ds(pl.multiple_of(8 * block, 8), 8)
        for comp in range(2):
            for k in range(3):
                dst[comp, k, at, :] = new[comp][k]
            for k in range(2):
                to = pl.multiple_of(8 * ((2 * comp + k) * count + block - start), 8)
                sent[pl.ds(to, 8), :] = new[comp][k] * inverse[k, at, :]
        return carry

    lax.fori_loop(start, start + count, last, 0, unroll=count)

    for comp in range(2):
        strip = [jnp.zeros((8, 128), jnp.float32)] * FOLD
        for n in range(count):
            g, place = divmod(n, FOLD)
            at = pl.ds(8 * (start + n), 8)
            tile = pltpu.roll(dst[comp, 2, at, :] * inverse[2, at, :], FIELD_RIM + 16 * g, 1)
            strip[place] = jnp.where((lane >= 16 * g) & (lane < 16 * g + 16), tile, strip[place])
        for place in range(FOLD):
            sent[pl.ds(32 * count + 8 * (FOLD * comp + place), 8), :] = strip[place]


def tail_kernel(rhs, matrix, inverse, once, twice, done, after, field, sent, second, third):
    edge = COUNTS[0]
    for ref in (second, third, field):
        clear_rims(ref)
    for comp in range(2):
        for k in range(3):
            for dst, src, low in ((second, twice, edge + 2), (third, once, edge)):
                for block in range(low, low + 3):
                    at = pl.ds(8 * block, 8)
                    dst[comp, k, at, :] = src[comp, k, at, :]
            for block in range(1, edge + 1):
                at = pl.ds(8 * block, 8)
                field[comp, k, at, :] = done[comp, k, at, :]
    step(once, second, rhs, matrix, edge + 5, INNER, INNER - edge - 4)
    step(second, third, rhs, matrix, edge + 3, INNER, INNER - edge - 2)
    send_part(1, third, field, sent, rhs, matrix, inverse)


def beside_terms(half, received, matrix, inverse, strips, store, ok=None):
    lane = lanes()
    start, count = STARTS[half], COUNTS[half]

    def read(at):
        return received[at, :] if ok is None else jnp.where(ok, received[at, :], 0.0)

    for comp in range(2):
        for n in range(count):
            g, place = divmod(n, FOLD)
            tile = read(pl.ds(32 * count + 8 * (FOLD * comp + place), 8))
            tile = pltpu.roll(tile, 128 - FIELD_RIM - 16 * g, 1)
            strips[comp, pl.ds(8 * n, 8), :] = jnp.where((lane < FIELD_RIM) | (lane >= 128 - FIELD_RIM), tile, 0.0)

    def body(n, carry):
        at = pl.ds(pl.multiple_of(8 * (start + n), 8), 8)
        for k in range(3):
            pair = []
            for comp in range(2):
                if k < 2:
                    value = read(pl.ds(pl.multiple_of(8 * ((2 * comp + k) * count + n), 8), 8))
                else:
                    value = strips[comp, pl.ds(pl.multiple_of(8 * n, 8), 8), :]
                pair.append(value * (inverse[k, at, :] * COUPLING))
            a, b, d = (matrix[i, k, at, :] for i in range(3))
            store(k, at, a * pair[0] - b * pair[1], d * pair[1] - b * pair[0])
        return carry

    lax.fori_loop(0, count, body, 0, unroll=count)


def carry_kernel(
    rhs, matrix, inverse, field, near_a, near_b, known, fresh,
    out, tensor,
    moved, work_a, work_b, strips, sems,
):
    inner = pl.ds(RIM, TILE)
    copies = [
        pltpu.make_async_copy(src.at[p, inner], tensor.at[base + p, 0], sems.at[base + p])
        for src, base, count in ((known, 0, 3), (fresh, 3, 2))
        for p in range(count)
    ]
    for copy in copies:
        copy.start()
    clear_rims(work_a)
    clear_rims(work_b)

    def store(k, at, x, y):
        moved[0, k, at, :] = rhs[0, k, at, :] + x
        moved[1, k, at, :] = rhs[1, k, at, :] + y

    for half, near in enumerate((near_a, near_b)):
        beside_terms(half, near, matrix, inverse, strips, store)
    step(field, work_a, moved, matrix)
    step(work_a, work_b, moved, matrix)
    step(work_b, work_a, moved, matrix)

    def last(block, carry):
        new = sweep(work_a, moved, matrix, block)
        at = pl.ds(pl.multiple_of(8 * block, 8), 8)
        for comp in range(2):
            for k in range(2):
                out[comp, k, at, :] = new[comp][k]
        return carry

    lax.fori_loop(2, BLOCKS - 2, last, 0, unroll=16)
    for copy in copies:
        copy.wait()


def second_kernel(half, matrix, inverse, carried, far, *rest):
    if half == 0:
        out, seam, moved, work_a, work_b, strips, result, sems = rest
    else:
        seam, _, out, moved, work_a, work_b, strips, result, sems = rest
    s = lax.axis_index("sec")
    inside = (s > 0) & (s < lax.axis_size("sec") - 1)
    edge = COUNTS[0]
    low, high = (1, edge + 1) if half == 0 else (edge, INNER)
    zero = jnp.zeros((8, 128), jnp.float32)
    for comp in range(2):
        for k in range(3):
            for ref in (moved, work_a, work_b):
                ref[comp, k, pl.ds(8 * low - 8, 8), :] = zero
                ref[comp, k, pl.ds(8 * high + 8, 8), :] = zero
            moved[comp, k, pl.ds(8 * (high if half == 0 else low), 8), :] = zero

    def store(k, at, x, y):
        moved[0, k, at, :] = x
        moved[1, k, at, :] = y

    beside_terms(half, far, matrix, inverse, strips, store, inside)
    step(moved, work_a, moved, matrix, low, high, high + 1 - low)
    step(work_a, work_b, moved, matrix, low, high, high + 1 - low)

    first, count = (2, edge - 2) if half == 0 else (edge, INNER - edge)
    moves = []

    def final(block, new):
        at = pl.ds(8 * block, 8)
        for comp in range(2):
            for k in range(2):
                value = new[comp][k] + carried[comp, k, at, :]
                if half == 1 and block <= edge + 1:
                    value = value + seam[comp, k, pl.ds(8 * (block - edge), 8), :]
                result[comp, pl.ds(8 * block - RIM, 8), pl.ds(128 * k, 128)] = value * inverse[k, at, :]

    for block in range(max(low, 2), min(high, BLOCKS - 3) + 1):
        new = sweep(work_b, moved, matrix, block)
        if block < first + count:
            final(block, new)
        else:
            for comp in range(2):
                for k in range(2):
                    seam[comp, k, pl.ds(8 * (block - edge), 8), :] = new[comp][k]
        if block + 1 == first + count or (block + 1 - first) % 8 == 0 and block < first + count:
            done = len(moves) // 2
            at = pl.ds(8 * (first + 8 * done) - RIM, 8 * (block + 1 - first - 8 * done))
            for c in range(2):
                moves.append(pltpu.make_async_copy(result.at[c, at], out.at[c, 0, at], sems.at[c, done]))
                moves[-1].start()
    for move in moves:
        move.wait()


def f32(*shape):
    return jax.ShapeDtypeStruct(shape, jnp.float32)


def vmem(*shape):
    return pltpu.VMEM(shape, jnp.float32)


def call(kernel, out_shape, args, mib=6, us=0, **rest):
    return pl.pallas_call(
        kernel,
        out_shape=out_shape,
        compiler_params=pltpu.CompilerParams(vmem_limit_bytes=mib << 20),
        cost_estimate=pl.CostEstimate(flops=us * 1000000, bytes_accessed=us * 3000000, transcendentals=0),
        **rest,
    )(*args)


def local(images, stiffness):
    grid = (3, EXT, 128)
    edge, strip = f32(2 * RIM, TILE), f32(2 * STRIP, 128)
    later_far = send(images, sec_odd)
    later_near = send(images, sec_even)
    in_hbm = pl.BlockSpec(memory_space=pltpu.HBM)
    tile = f32(1, TILE, TILE)
    held = [pltpu.with_memory_space_constraint(x, pltpu.HBM) for x in (images, stiffness)]
    to_o, to_e = call(
        edges_kernel,
        (edge, edge),
        held,
        us=1,
        in_specs=[in_hbm, in_hbm],
        scratch_shapes=[vmem(2 * RIM, TILE), vmem(2 * RIM, TILE), pltpu.SemaphoreType.DMA((2, 2))],
    )
    images, stiffness = call(
        load_kernel,
        (tile, tile),
        (*held, to_o),
        us=1,
        in_specs=[in_hbm, in_hbm, pl.BlockSpec(memory_space=pltpu.VMEM)],
        scratch_shapes=[pltpu.SemaphoreType.DMA((2, CUTS))],
    )
    row_o = send(to_o, row_odd)
    row_e = send(to_e, row_even)

    strip_o, strip_e = call(strip_kernel, (strip, strip), (images, stiffness, row_o, row_e))
    col_o = send(strip_o, col_odd)
    col_e = send(strip_e, col_even)

    band = call(band_kernel, f32(3 * 128, 3 * 128), (to_o,), us=1)

    rims = call(rims_kernel, f32(RIMS, 128), (row_o, row_e, col_o, col_e))
    rims_far = send(rims, sec_odd)
    rims_near = send(rims, sec_even)
    ext, gx, gy, matrix, inverse, known = call(
        matrix_kernel,
        (f32(3, EXT + 16, 128), f32(*grid), f32(*grid), f32(3, *grid), f32(*grid), f32(3, EXT, TILE)),
        (images, stiffness, row_o, row_e, col_o, col_e, band),
        mib=20,
        us=4,
        scratch_shapes=[vmem(*grid), vmem(3, *grid), vmem(3 * EXT, 3 * 128)],
    )
    fresh, rhs, twice, once, done, sent_a = call(
        first_kernel,
        (f32(2, EXT, TILE), *[f32(2, *grid)] * 4, f32(SENT[0], 128)),
        (ext, gx, gy, matrix, inverse, later_far, later_near, rims_far, rims_near, band),
        mib=20,
        us=5,
        scratch_shapes=[vmem(*grid), vmem(2, *grid), vmem(2 * EXT, 3 * 128)],
    )

    far_a = send(sent_a, sec_odd)
    near_a = send(sent_a, sec_even)
    field, sent_b = call(
        tail_kernel,
        (f32(2, *grid), f32(SENT[1], 128)),
        (rhs, matrix, inverse, once, twice, done, near_a),
        mib=16,
        us=1,
        scratch_shapes=[vmem(2, *grid), vmem(2, *grid)],
    )
    far_b = send(sent_b, sec_odd)
    near_b = send(sent_b, sec_even)
    whole = pl.BlockSpec(memory_space=pltpu.VMEM)
    anywhere = pl.BlockSpec(memory_space=pl.ANY)
    carried, tensor = call(
        carry_kernel,
        (f32(2, 2, EXT, 128), f32(5, 1, TILE, TILE)),
        (rhs, matrix, inverse, field, near_a, near_b, known, fresh),
        mib=16,
        us=3,
        out_specs=[whole, anywhere],
        scratch_shapes=[
            vmem(2, *grid),
            vmem(2, *grid),
            vmem(2, *grid),
            vmem(2, 8 * max(COUNTS), 128),
            pltpu.SemaphoreType.DMA((5,)),
        ],
    )
    final = f32(2, 1, TILE, TILE)
    scratch = [
        vmem(2, *grid),
        vmem(2, *grid),
        vmem(2, *grid),
        vmem(2, 8 * max(COUNTS), 128),
        vmem(2, TILE, TILE),
        pltpu.SemaphoreType.DMA((2, CUTS)),
    ]
    field, seam = call(
        functools.partial(second_kernel, 0),
        (final, f32(2, 2, 16, 128)),
        (matrix, inverse, carried, far_a),
        mib=16,
        us=2,
        out_specs=[anywhere, whole],
        scratch_shapes=scratch,
    )
    field = call(
        functools.partial(second_kernel, 1),
        final,
        (matrix, inverse, carried, far_b, seam, field),
        mib=16,
        us=2,
        in_specs=[whole] * 5 + [anywhere],
        out_specs=anywhere,
        input_output_aliases={5: 0},
        scratch_shapes=scratch,
    )
    return tensor, field


def solution(mesh):
    in_specs = (P("sec", "row", "col"), P("sec", "row", "col"))
    out_specs = (P(None, "sec", "row", "col"), P(None, "sec", "row", "col"))
    return jax.shard_map(local, mesh=mesh, in_specs=in_specs, out_specs=out_specs, check_vma=False)
```
